256 devices in a mesh: section: 8 (over x, core), dp: 32 (over y, z).
Axes of the slice: x: 4, y: 4, z: 8, core: 2. Of those that a mesh axis runs over, the one named last changes fastest.
Arguments:
- section_inputs: bfloat16 [8, 8, 1024, 8192], P('section', None, 'dp'), may hold values from -6 to 6
- adapter_down: bfloat16 [8, 8192, 128], P('section'), may hold values from -0.0625 to 0.0625
- adapter_up: bfloat16 [8, 8192, 128], P('section'), may hold values from -0.5 to 0.5
- representation: bfloat16 [8, 1024, 8192], P('section', 'dp'), may hold values from -6 to 6
- head_weights: bfloat16 [8192, 128], P('dp'), may hold values from -1 to 1
- head_targets: bfloat16 [8, 1024, 128], P('section', 'dp'), may hold values from -40 to 40
- head_task: int32 [8, 1], replicated, may hold values from 0 to 5
Outputs:
- down_grads: float32 [8, 8192, 128], P('section', 'dp')
- up_grads: float32 [8, 8192, 128], P('section', 'dp')
- task_weights: float32 [6], replicated
The draws below stay inside these ranges and needn't reach their ends.
Inputs may be any that keep to these rules, and one draw needn't show every extreme that they name: `head_task`: each head belongs to one task, and every task has at least one head.
All inputs are finite; a program needn't handle non-finite values.
Results may differ from the reference program's by a relative error of at most 0.022.
Values may be sent and summed in bfloat16 or wider, within the bound.
No kernel may reach another device: no remote copies, remote signals or barrier semaphores. Data moves between devices by JAX's collectives and lax.ppermute only.
A program may use at most 64 MiB of HBM per device.

```python
import jax
import jax.numpy as jnp
from jax import lax

D = 8192
RANK = 128
HEADS = 8
HEAD_OUT = 16
TASKS = 6
STEPS = 20
MICRO = 8
TOKENS = 1024
N_SECTION = 8


def draw_head_weights(key, part):
    key_common, key_own = jax.random.split(key)
    columns = HEADS * HEAD_OUT
    common = jax.random.normal(key_common, (D, HEAD_OUT), jnp.float32)
    own_part = jax.random.normal(key_own, (D, columns), jnp.float32)
    tiled_common = jnp.tile(common, (1, HEADS))
    values = (0.8 * tiled_common + 0.6 * own_part) / jnp.sqrt(jnp.float32(D))
    return jnp.clip(values, -1.0, 1.0).astype(jnp.bfloat16)


def draw_head_targets(key, part):
    subkeys = jax.random.split(key, 4)
    columns = HEADS * HEAD_OUT
    full_shape = (MICRO, TOKENS, columns)
    position = (jnp.arange(MICRO * TOKENS, dtype=jnp.float32) / (MICRO * TOKENS)).reshape(MICRO, TOKENS, 1)
    rising = 0.5 * jnp.exp(jnp.log(4.0) * position)
    token_scale = jnp.exp(jax.random.uniform(subkeys[0], (MICRO, TOKENS, 1), jnp.float32, -0.693, 0.693))
    shared = jax.random.normal(subkeys[1], (MICRO, TOKENS, HEAD_OUT), jnp.float32)
    own_part = jax.random.normal(subkeys[2], full_shape, jnp.float32)
    column_scale = jnp.exp(jax.random.uniform(subkeys[3], (1, 1, columns), jnp.float32, -0.693, 0.693))
    values = rising * token_scale * column_scale * (0.6 * jnp.tile(shared, (1, 1, HEADS)) + 0.8 * own_part)
    return jnp.clip(values, -40.0, 40.0).astype(jnp.bfloat16)


def block_scale(stream_key, shape, cuts, least, high):
    factor_of = 1.0
    for dim, shards_of in cuts:
        draws = jax.random.uniform(jax.random.fold_in(jax.random.fold_in(stream_key, 6), dim), (shards_of,), jnp.float32, least / len(cuts), high / len(cuts))
        factor_of = factor_of * jnp.repeat(jnp.exp(draws), shape[dim] // shards_of).reshape((-1,) + (1,) * (len(shape) - 1 - dim))
    return factor_of


def different_ones(stream_key, rows, amount, top, lift):
    sequence = jax.random.permutation(jax.random.fold_in(stream_key, 1), amount)
    boost = sequence
    for power in range(3):
        boost = boost * boost // amount
    boost = boost * lift // amount
    tickets = jax.random.randint(jax.random.fold_in(stream_key, 2), (rows, amount), 0, 4096) + boost
    sure = jax.random.permutation(jax.random.fold_in(stream_key, 3), rows)[jnp.arange(amount) % rows]
    tickets = jnp.where(jnp.arange(rows)[:, None] == sure[None, :], 1 << 14, tickets)
    merit = tickets * amount + jnp.arange(amount)
    return lax.top_k(merit.astype(jnp.int32), top)[1].astype(jnp.int32)


def noise(stream_key, shape, width, most, cuts=(), kind=jnp.bfloat16):
    array = width * jax.random.normal(stream_key, shape, jnp.float32)
    if cuts:
        array = array * block_scale(stream_key, shape, cuts, -0.22, 0.18)
    return jnp.clip(array, -most, most).astype(kind)


def setup_inputs(seed: int = 0) -> dict:
    arg_keys = jax.random.split(jax.random.key(seed), 8)
    section_inputs = noise(arg_keys[0], (N_SECTION, MICRO, TOKENS, D), 1.0, 6.0, ((0, 8), (2, 32)))
    adapter_down = noise(arg_keys[1], (N_SECTION, D, RANK), D ** -0.5, 0.0625, ((0, 8),))
    adapter_up = noise(arg_keys[2], (N_SECTION, D, RANK), RANK ** -0.5, 0.5, ((0, 8),))
    representation = noise(arg_keys[3], (MICRO, TOKENS, D), 1.0, 6.0, ((0, 8), (1, 32)))
    head_weights = draw_head_weights(jax.random.fold_in(arg_keys[7], 71), 0)
    head_targets = draw_head_targets(jax.random.fold_in(arg_keys[7], 71), 0)
    head_task = different_ones(arg_keys[6], HEADS, TASKS, 1, 0)
    return {"section_inputs": section_inputs, "adapter_down": adapter_down, "adapter_up": adapter_up, "representation": representation, "head_weights": head_weights, "head_targets": head_targets, "head_task": head_task}


STEP_RATE = 3.0


def swish_slope(preact):
    logistic = jax.nn.sigmoid(preact)
    return logistic * (1.0 + preact * (1.0 - logistic))


def task_matrix(head_task):
    column_task = jnp.repeat(head_task[:, 0], HEAD_OUT)
    return (column_task[None, :] == jnp.arange(TASKS, dtype=jnp.int32)[:, None]).astype(jnp.float32)


def descend(gram_matrix):
    trace_sum = jnp.trace(gram_matrix) + 1e-6
    start = jnp.full((TASKS,), 1.0 / TASKS, dtype=jnp.float32)

    def advance(counter, weights):
        descent = jnp.dot(gram_matrix, weights, precision=lax.Precision.HIGHEST) / trace_sum
        weights = weights * jnp.exp(-STEP_RATE * descent)
        return weights / jnp.sum(weights)

    return lax.fori_loop(0, STEPS, advance, start)


def section_back(inputs, down_map, up_map, cotangent):
    preact = jnp.dot(inputs, down_map, preferred_element_type=jnp.float32)
    active = jax.nn.silu(preact).astype(jnp.bfloat16)
    branch = jnp.dot(cotangent, up_map, preferred_element_type=jnp.float32)
    inner = (branch * swish_slope(preact)).astype(jnp.bfloat16)
    back = lax.dot_general(inner, down_map, (((1,), (1,)), ((), ())), preferred_element_type=jnp.float32)
    passed = (cotangent.astype(jnp.float32) + back).astype(jnp.bfloat16)
    return active, inner, passed


def reference(section_inputs, adapter_down, adapter_up, representation, head_weights, head_targets, head_task):
    onehot = task_matrix(head_task)
    residuals = []
    gram_matrix = jnp.zeros((TASKS, TASKS), jnp.float32)
    for micro_index in range(MICRO):
        predicted = jnp.dot(representation[micro_index], head_weights, preferred_element_type=jnp.float32)
        residual = (predicted - head_targets[micro_index].astype(jnp.float32)).astype(jnp.bfloat16)
        residuals.append(residual)
        task_grads = jnp.stack([lax.dot_general(residual * onehot[task_index].astype(jnp.bfloat16), head_weights, (((1,), (1,)), ((), ())), preferred_element_type=jnp.float32) for task_index in range(TASKS)])
        gram_matrix = gram_matrix + jnp.einsum('atd,btd->ab', task_grads, task_grads, precision=lax.Precision.HIGHEST)
    mixing = descend(gram_matrix)
    column_weight = jnp.dot(mixing, onehot, precision=lax.Precision.HIGHEST)
    cotangents = []
    for residual in residuals:
        weighted = (residual.astype(jnp.float32) * column_weight[None, :]).astype(jnp.bfloat16)
        cotangents.append(lax.dot_general(weighted, head_weights, (((1,), (1,)), ((), ())), preferred_element_type=jnp.float32).astype(jnp.bfloat16))
    down_list = []
    up_list = []
    for section_index in range(N_SECTION - 1, -1, -1):
        grad_down = jnp.zeros((D, RANK), jnp.float32)
        grad_up = jnp.zeros((D, RANK), jnp.float32)
        for micro_index in range(MICRO):
            inputs = section_inputs[section_index, micro_index]
            current = cotangents[micro_index]
            active, inner, passed = section_back(inputs, adapter_down[section_index], adapter_up[section_index], current)
            grad_down = grad_down + jnp.dot(inputs.T, inner, preferred_element_type=jnp.float32)
            grad_up = grad_up + jnp.dot(current.T, active, preferred_element_type=jnp.float32)
            cotangents[micro_index] = passed
        down_list.insert(0, grad_down)
        up_list.insert(0, grad_up)
    return jnp.stack(down_list), jnp.stack(up_list), mixing
```

```python
import jax
import jax.numpy as jnp
from jax import lax
from jax.experimental import pallas as pl
from jax.experimental.pallas import tpu as pltpu
from jax.sharding import Mesh
from jax.sharding import PartitionSpec as P

HEAD_OUT = 16
TASKS = 6
STEPS = 20
STEP_RATE = 3.0
NX = 4
NC = 2
NY = 4
NZ = 8
SECTIONS = NX * NC
DP = NY * NZ
BF16 = jnp.bfloat16
F32 = jnp.float32


def shift(value, axis, steps):
    count = lax.axis_size(axis)
    return lax.ppermute(value, axis, [(src, (src + steps) % count) for src in range(count)])


def gather_x(value):
    return jnp.stack([value] + [shift(value, "x", -k) for k in range(1, NX)])


def swap_c(value):
    return lax.ppermute(value, "c", [(0, 1), (1, 0)])


def exchange_dp(blocks):
    return lax.all_to_all(blocks, ("y", "z"), 0, 0, tiled=True)


def gather_dp(block):
    return exchange_dp(jnp.broadcast_to(block[None], (DP,) + block.shape))


def split_hi_lo(value):
    high = value.astype(BF16)
    low = (value - high.astype(F32)).astype(BF16)
    return jnp.concatenate([high, low], axis=0)


def col_slot(stage, column):
    if stage == column:
        return 0
    away = (stage // NC - column // NC) % NX
    return (NX if stage % NC != column % NC else 0) + away


def chain_kernel(
    where_ref, gram_ref, mask_ref, own_ref, other_ref, slope_own_ref, slope_other_ref,
    left_ref, inner_ref, mix_ref,
):
    my_x = where_ref[0]
    my_c = where_ref[1]
    my_stage = my_x * NC + my_c
    gram = gram_ref[...]
    rows = lax.broadcasted_iota(jnp.int32, gram.shape, 0)
    lanes = lax.broadcasted_iota(jnp.int32, gram.shape, 1)
    diagonal = jnp.where(rows == lanes, gram, 0.0)
    trace_sum = jnp.sum(jnp.sum(diagonal, axis=1, keepdims=True), axis=0, keepdims=True) + 1e-06
    scaled = gram / trace_sum
    down0 = jnp.where(rows < TASKS, 1.0 / TASKS, 0.0)
    along0 = jnp.where(lanes < TASKS, 1.0 / TASKS, 0.0)

    def advance(counter, carry):
        down, along = carry
        step_down = jnp.sum(scaled * along, axis=1, keepdims=True)
        step_along = jnp.sum(scaled * down, axis=0, keepdims=True)
        total = jnp.sum(along[0:1], axis=1, keepdims=True)
        rate = -STEP_RATE / total
        down = down * jnp.exp(rate * step_down)
        along = along * jnp.exp(rate * step_along)
        return down, along

    down, along = lax.fori_loop(0, STEPS, advance, (down0, along0))
    total_along = jnp.sum(along[0:1], axis=1, keepdims=True)
    total_down = jnp.sum(down, axis=0, keepdims=True)
    mix_ref[...] = along / total_along
    column_weight = jnp.sum((down / total_down) * mask_ref[...], axis=0, keepdims=True)

    def pick(own, other, stage, lo, size):
        slot = (stage // NC - my_x) % NX
        same = my_c == stage % NC
        return jnp.where(same, own[slot, lo : lo + size, :], other[slot, lo : lo + size, :])

    tok = 32
    parts = [
        (pick(own_ref, other_ref, stage, 1024, tok).astype(F32) * column_weight).astype(BF16)
        for stage in range(SECTIONS)
    ]
    weighted = jnp.concatenate(parts, axis=0)
    left_ref[0] = weighted
    inners = {}
    for stage in range(SECTIONS - 1, -1, -1):
        sources = [(weighted, stage)] + [(inners[s], s) for s in range(stage + 1, SECTIONS)]
        branch = None
        for value, s in sources:
            block = pick(own_ref, other_ref, stage, 128 * col_slot(s, stage), 128)
            term = jnp.dot(value, block, preferred_element_type=F32)
            branch = term if branch is None else branch + term
        slope = pick(slope_own_ref, slope_other_ref, stage, 256, 256)
        inner = (branch * slope.astype(F32)).astype(BF16)
        inners[stage] = inner
        slot = (stage // NC - my_x) % NX + jnp.where(my_c == stage % NC, 0, NX)

        @pl.when(stage == my_stage)
        def _():
            inner_ref[...] = inner

        @pl.when(stage != my_stage)
        def _():
            left_ref[slot] = jnp.where(stage > my_stage, inner, jnp.zeros_like(inner))


def run_chain(where, gram, mask, own, other, slope_own, slope_other):
    tokens = 256
    vmem = pl.BlockSpec(memory_space=pltpu.VMEM)
    return pl.pallas_call(
        chain_kernel,
        out_shape=(
            jax.ShapeDtypeStruct((SECTIONS, tokens, 128), BF16),
            jax.ShapeDtypeStruct((tokens, 128), BF16),
            jax.ShapeDtypeStruct((8, 128), F32),
        ),
        in_specs=[pl.BlockSpec(memory_space=pltpu.SMEM)] + [vmem] * 6,
        out_specs=(vmem, vmem, vmem),
        name="mix_chain",
    )(where, gram, mask, own, other, slope_own, slope_other)


def body(
    section_inputs, adapter_down, adapter_up, representation, head_weights, head_targets, head_task
):
    my_x = lax.axis_index("x")
    my_c = lax.axis_index("c")
    my_dp = lax.axis_index("y") * NZ + lax.axis_index("z")
    dim_model = section_inputs.shape[3]
    saved = section_inputs[0].reshape(-1, dim_model)
    down_map = adapter_down[0]
    up_map = adapter_up[0]
    heads = head_weights
    share = heads.shape[0]
    rank = heads.shape[1]

    preact = jnp.dot(saved, down_map, preferred_element_type=F32)
    logistic = jax.nn.sigmoid(preact)
    active = (preact * logistic).astype(BF16)
    slope = (logistic * (1.0 + preact * (1.0 - logistic))).astype(BF16)

    down_rows = lax.dynamic_slice_in_dim(down_map, my_dp * share, share, 0)
    near = gather_x(jnp.concatenate([down_rows, slope], axis=0))
    far = swap_c(near)
    factors = jnp.concatenate([heads[None], near[1:, :share], far[:, :share]], axis=0)
    up_rows = lax.dynamic_slice_in_dim(up_map, my_dp * share, share, 0)
    part_cross = lax.dot_general(
        factors, up_rows, (((1,), (0,)), ((), ())), preferred_element_type=F32
    ).astype(BF16)

    half = share // NC
    head_half = lax.dynamic_slice_in_dim(heads, my_c * half, half, 0)
    sent = jnp.concatenate(
        [
            jnp.broadcast_to(head_half[None], (DP, half, rank)),
            part_cross.reshape(DP, -1, rank),
        ],
        axis=1,
    )
    got = exchange_dp(sent)
    mine = got[:, :half]
    cross_rows = jnp.sum(got[:, half:].astype(F32), axis=0).astype(BF16)
    theirs = swap_c(mine)
    first = jnp.where(my_c == 0, mine, theirs)
    second = jnp.where(my_c == 0, theirs, mine)
    weights = jnp.concatenate([first, second], axis=1).reshape(dim_model, rank)

    predicted = jnp.dot(representation[0], weights, preferred_element_type=F32)
    residual = (predicted - head_targets[0].astype(F32)).astype(BF16)
    head_gram = lax.dot_general(
        weights, weights, (((0,), (0,)), ((), ())), preferred_element_type=F32
    )
    residual_gram = lax.dot_general(
        residual, residual, (((0,), (0,)), ((), ())), preferred_element_type=F32
    )
    column_task = jnp.repeat(head_task[:, 0], HEAD_OUT)
    mask = (column_task[None, :] == jnp.arange(8, dtype=jnp.int32)[:, None]).astype(F32)
    product = head_gram * residual_gram
    high = lax.Precision.HIGHEST
    part_gram = jnp.dot(mask, jnp.dot(product, mask.T, precision=high), precision=high)
    part_gram = jnp.pad(part_gram, ((0, 0), (0, rank - 8)))

    got = gather_dp(jnp.concatenate([cross_rows, split_hi_lo(part_gram)], axis=0))
    cross = got[:, :32].reshape(-1, rank)
    gram_stage = jnp.sum(got[:, 32:].astype(F32), axis=0)
    gram_stage = gram_stage[:8] + gram_stage[8:]
    payload = jnp.concatenate([cross, residual, split_hi_lo(gram_stage)], axis=0)
    own = gather_x(payload)
    other = swap_c(own)
    gram = jnp.sum(own[:, 1056:].astype(F32) + other[:, 1056:].astype(F32), axis=0)
    gram = gram[:8] + gram[8:]

    where = jnp.stack([my_x, my_c]).astype(jnp.int32)
    left, inner, mix = run_chain(where, gram, mask, own, other, near, far)

    part_down = lax.dot_general(
        saved, inner, (((0,), (0,)), ((), ())), preferred_element_type=F32
    ).astype(BF16)
    blocks = part_down.reshape(NY, NZ * share, rank)
    my_y = lax.axis_index("y")
    total = lax.dynamic_index_in_dim(blocks, my_y, 0, keepdims=False).astype(F32)
    for k in range(1, NY):
        block = lax.dynamic_index_in_dim(blocks, (my_y + k) % NY, 0, keepdims=False)
        total = total + shift(block, "y", k).astype(F32)

    part_mid = lax.dot_general(
        left, active, (((1,), (0,)), ((), ())), preferred_element_type=F32
    ).astype(BF16)
    got = exchange_dp(part_mid.reshape(DP, -1, rank))
    mid_rows = jnp.sum(got.astype(F32), axis=0).astype(BF16)
    middle = gather_dp(mid_rows).reshape(SECTIONS, rank, rank)
    grad_up = lax.dot_general(
        factors, middle, (((0, 2), (0, 1)), ((), ())), preferred_element_type=F32
    )

    got = lax.all_to_all(
        total.astype(BF16).reshape(NZ, share, rank), "z", 0, 0, tiled=True
    )
    grad_down = jnp.sum(got.astype(F32), axis=0)
    return (grad_down[None], grad_up[None], mix[0, :TASKS])


def solution(mesh):
    fine = Mesh(mesh.devices.reshape(NX, NC, NY, NZ), ("x", "c", "y", "z"))
    section = ("x", "c")
    dp = ("y", "z")
    in_specs = (
        P(section, None, dp, None),
        P(section, None, None),
        P(section, None, None),
        P(section, dp, None),
        P(dp, None),
        P(section, dp, None),
        P(),
    )
    out_specs = (P(section, dp, None), P(section, dp, None), P())
    return jax.shard_map(body, mesh=fine, in_specs=in_specs, out_specs=out_specs, check_vma=False)
```

```python
import jax
import jax.numpy as jnp
from jax import lax
from jax.experimental import pallas as pl
from jax.experimental.pallas import tpu as pltpu
from jax.sharding import Mesh
from jax.sharding import PartitionSpec as P

HEAD_OUT = 16
TASKS = 6
STEPS = 20
STEP_RATE = 3.0
NX = 4
NC = 2
NY = 4
NZ = 8
SECTIONS = NX * NC
DP = NY * NZ
BF16 = jnp.bfloat16
F32 = jnp.float32


def shift(value, axis, steps):
    count = lax.axis_size(axis)
    return lax.ppermute(value, axis, [(src, (src + steps) % count) for src in range(count)])


def swap_c(value):
    return lax.ppermute(value, "c", [(0, 1), (1, 0)])


def gather_x(value):
    return [value] + [shift(value, "x", -k) for k in range(1, NX)]


def gather_section(value):
    near = jnp.stack(gather_x(value))
    return near, swap_c(near)


def exchange_dp(blocks):
    return lax.all_to_all(blocks, ("y", "z"), 0, 0, tiled=True)


def gather_dp(block):
    return exchange_dp(jnp.broadcast_to(block[None], (DP,) + block.shape))


def at(value, index):
    return lax.dynamic_index_in_dim(value, index, 0, keepdims=False)


def rows_at(value, start, size):
    return lax.dynamic_slice_in_dim(value, start, size, 0)


def col_slot(stage, column):
    if stage == column:
        return 0
    away = (stage // NC - column // NC) % NX
    return (NX if stage % NC != column % NC else 0) + away


def across(left, right):
    return lax.dot_general(left, right, (((0,), (0,)), ((), ())), preferred_element_type=F32)


def chain_kernel(
    where_ref, gram_ref, mask_ref, residual_ref, active_ref, own_ref, other_ref,
    slope_own_ref, slope_other_ref, middle_ref, inner_ref, mix_ref,
):
    my_x = where_ref[0]
    my_c = where_ref[1]
    my_stage = my_x * NC + my_c
    gram = jnp.sum(gram_ref[...], axis=0)
    rows = lax.broadcasted_iota(jnp.int32, gram.shape, 0)
    lanes = lax.broadcasted_iota(jnp.int32, gram.shape, 1)
    diagonal = jnp.where(rows == lanes, gram, 0.0)
    trace_sum = jnp.sum(jnp.sum(diagonal, axis=1, keepdims=True), axis=0, keepdims=True) + 1e-06
    scaled = gram / trace_sum
    down0 = jnp.where(rows < TASKS, 1.0 / TASKS, 0.0)
    along0 = jnp.where(lanes < TASKS, 1.0 / TASKS, 0.0)

    def advance(counter, carry):
        down, along = carry
        step_down = jnp.sum(scaled * along, axis=1, keepdims=True)
        step_along = jnp.sum(scaled * down, axis=0, keepdims=True)
        total = jnp.sum(along[0:1], axis=1, keepdims=True)
        rate = -STEP_RATE / total
        down = down * jnp.exp(rate * step_down)
        along = along * jnp.exp(rate * step_along)
        return down, along

    down, along = lax.fori_loop(0, STEPS, advance, (down0, along0))
    total_along = jnp.sum(along[0:1], axis=1, keepdims=True)
    total_down = jnp.sum(down, axis=0, keepdims=True)
    mix_ref[...] = along / total_along
    column_weight = jnp.sum((down / total_down) * mask_ref[...], axis=0, keepdims=True)

    def pick(own, other, stage, lo, size):
        slot = (stage // NC - my_x) % NX
        same = my_c == stage % NC
        return jnp.where(same, own[slot, lo : lo + size, :], other[slot, lo : lo + size, :])

    active = active_ref[...]
    weighted = (residual_ref[...].astype(F32) * column_weight).astype(BF16)
    middle_ref[0] = across(weighted, active).astype(BF16)
    inners = {}
    for stage in range(SECTIONS - 1, -1, -1):
        sources = [(weighted, stage)] + [(inners[s], s) for s in range(stage + 1, SECTIONS)]
        branch = None
        for value, s in sources:
            block = pick(own_ref, other_ref, stage, 128 * col_slot(s, stage), 128)
            term = jnp.dot(value, block, preferred_element_type=F32)
            branch = term if branch is None else branch + term
        slope = pick(slope_own_ref, slope_other_ref, stage, 0, 256)
        inner = (branch * slope.astype(F32)).astype(BF16)
        inners[stage] = inner

        @pl.when(stage == my_stage)
        def _():
            inner_ref[...] = inner

    for stage in range(SECTIONS):
        slot = (stage // NC - my_x) % NX + jnp.where(my_c == stage % NC, 0, NX)
        product = across(inners[stage], active)

        @pl.when(stage != my_stage)
        def _():
            middle_ref[slot] = jnp.where(stage > my_stage, product, 0.0).astype(BF16)


def run_chain(*operands):
    vmem = pl.BlockSpec(memory_space=pltpu.VMEM)
    return pl.pallas_call(
        chain_kernel,
        out_shape=(
            jax.ShapeDtypeStruct((SECTIONS, 128, 128), BF16),
            jax.ShapeDtypeStruct((256, 128), BF16),
            jax.ShapeDtypeStruct((8, 128), F32),
        ),
        in_specs=[pl.BlockSpec(memory_space=pltpu.SMEM)] + [vmem] * (len(operands) - 1),
        out_specs=(vmem, vmem, vmem),
        name="mix_chain",
    )(*operands)


def down_kernel(y_ref, *refs):
    inputs = refs[:NY]
    inners = refs[NY : 2 * NY]
    out_ref = refs[2 * NY]
    total = across(inners[0][...], inputs[0][...])
    for k in range(1, NY):
        total = total + across(inners[k][...], inputs[k][...])
    total = total.astype(BF16)
    for j in range(2):
        out_ref[j] = total[:, 256 * j : 256 * (j + 1)]


def run_down(my_y, saved, received, inners):
    tokens = saved.shape[0]
    cols = 512
    steps = received[0].shape[1] // cols
    whole = pl.BlockSpec((tokens, 128), lambda i, y: (0, 0))
    return pl.pallas_call(
        down_kernel,
        grid_spec=pltpu.PrefetchScalarGridSpec(
            num_scalar_prefetch=1,
            grid=(steps,),
            in_specs=[pl.BlockSpec((tokens, cols), lambda i, y: (0, y[0] * steps + i))]
            + [pl.BlockSpec((tokens, cols), lambda i, y: (0, i))] * (NY - 1)
            + [whole] * NY,
            out_specs=pl.BlockSpec((2, 128, 256), lambda i, y: (i, 0, 0)),
        ),
        out_shape=jax.ShapeDtypeStruct((NZ, 128, 256), BF16),
        name="down_product",
    )(my_y.reshape(1), saved, *received, *inners)


def body(
    section_inputs, adapter_down, adapter_up, representation, head_weights, head_targets, head_task
):
    my_x = lax.axis_index("x")
    my_c = lax.axis_index("c")
    my_y = lax.axis_index("y")
    my_dp = my_y * NZ + lax.axis_index("z")
    my_stage = my_x * NC + my_c
    dim_model = section_inputs.shape[3]
    saved = section_inputs[0].reshape(-1, dim_model)
    down_map = adapter_down[0]
    up_map = adapter_up[0]
    heads = head_weights
    share, rank = heads.shape
    tok = representation.shape[1]

    piece = rows_at(heads, my_c * 128 + my_x * 32, 32)
    turn = [(a * NY + b, b * NY + a) for a in range(NX) for b in range(NY)]
    piece = lax.ppermute(piece, ("x", "y"), turn)

    blocks = representation[0].reshape(tok, NX, NZ, NC, 128).transpose(3, 1, 2, 0, 4)
    keep = at(blocks, my_c)
    swapped = swap_c(at(blocks, 1 - my_c))
    pair = jnp.stack([keep, swapped], axis=1)
    down_rows = rows_at(down_map, my_dp * share, share)
    near_rep = [at(pair, my_x)]
    near_down = [down_rows]
    for k in range(1, NX):
        sent = jnp.concatenate([at(pair, (my_x - k) % NX).reshape(-1, 128), down_rows], axis=0)
        got = shift(sent, "x", -k)
        near_rep.append(got[: 2 * NZ * tok].reshape(NC, NZ, tok, 128))
        near_down.append(got[2 * NZ * tok :])
    near = jnp.stack(near_down)
    far = swap_c(near)
    factors = jnp.concatenate([heads[None], near[1:], far], axis=0)
    up_rows = rows_at(up_map, my_dp * share, share)
    part_cross = lax.dot_general(
        factors, up_rows, (((1,), (0,)), ((), ())), preferred_element_type=F32
    ).astype(BF16)

    preact = jnp.dot(saved, down_map, preferred_element_type=F32)
    logistic = jax.nn.sigmoid(preact)
    active = (preact * logistic).astype(BF16)
    slope = (logistic * (1.0 + preact * (1.0 - logistic))).astype(BF16)
    slope_own, slope_other = gather_section(slope)

    wide = dim_model // NY
    received = []
    for k in range(1, NY):
        cut = lax.dynamic_slice_in_dim(saved, ((my_y - k) % NY) * wide, wide, 1)
        received.append(shift(cut, "y", -k))

    got = exchange_dp(
        jnp.concatenate(
            [jnp.broadcast_to(piece[None], (DP, 32, rank)), part_cross.reshape(DP, 32, rank)],
            axis=1,
        )
    )
    head_part = got[:, :32].reshape(NY, NZ, 32, rank).transpose(1, 0, 2, 3)
    head_part = head_part.reshape(NZ, 128, rank)
    cross_rows = jnp.sum(got[:, 32:].astype(F32), axis=0).astype(BF16)
    cross = gather_dp(cross_rows).reshape(-1, rank)

    rep_part = jnp.stack(near_rep)
    part = lax.dot_general(
        rep_part, head_part, (((2, 4), (0, 1)), ((), ())), preferred_element_type=F32
    )
    part = jnp.where(my_c == 0, part, part[:, ::-1])
    part = rows_at(jnp.concatenate([part, part], axis=0), (NX - my_x) % NX, NX)
    part = part.reshape(SECTIONS, tok, rank)
    is_mine = (jnp.arange(SECTIONS) == my_stage)[:, None, None]
    part = part - jnp.where(is_mine, head_targets.astype(F32), 0.0)
    flat = head_part.reshape(-1, rank)
    part = jnp.concatenate([part.reshape(-1, rank), across(flat, flat)], axis=0)
    part = part + swap_c(part)
    first, second, third, fourth = gather_x(part)
    part = (first + third) + (second + fourth)
    residual = part[: SECTIONS * tok].astype(BF16)
    head_gram = part[SECTIONS * tok :]

    column_task = jnp.repeat(head_task[:, 0], HEAD_OUT)
    mask = (column_task[None, :] == jnp.arange(8, dtype=jnp.int32)[:, None]).astype(F32)
    product = head_gram * across(residual, residual)
    high = lax.Precision.HIGHEST
    part_gram = jnp.dot(mask, jnp.dot(product, mask.T, precision=high), precision=high)
    part_gram = jnp.pad(part_gram, ((0, 0), (0, rank - 8)))
    cross_own, cross_other = gather_section(cross)
    gram = gather_dp(part_gram)

    where = jnp.stack([my_x, my_c]).astype(jnp.int32)
    middle, inner, mix = run_chain(
        where, gram, mask, residual, active, cross_own, cross_other, slope_own, slope_other
    )

    got = exchange_dp(middle.reshape(DP, 32, rank))
    inners = [inner] + [shift(inner, "y", -k) for k in range(1, NY)]
    part_down = run_down(my_y, saved, received, inners)
    got_down = lax.all_to_all(part_down, "z", 0, 0, tiled=True)
    middle = gather_dp(jnp.sum(got.astype(F32), axis=0).astype(BF16))
    middle = middle.reshape(SECTIONS, rank, rank)
    grad_up = lax.dot_general(
        factors, middle, (((0, 2), (0, 1)), ((), ())), preferred_element_type=F32
    )
    grad_down = jnp.sum(got_down.astype(F32), axis=0).T
    return (grad_down[None], grad_up[None], mix[0, :TASKS])


def solution(mesh):
    fine = Mesh(mesh.devices.reshape(NX, NC, NY, NZ), ("x", "c", "y", "z"))
    section = ("x", "c")
    dp = ("y", "z")
    in_specs = (
        P(section, None, dp, None),
        P(section, None, None),
        P(section, None, None),
        P(section, dp, None),
        P(dp, None),
        P(section, dp, None),
        P(),
    )
    out_specs = (P(section, dp, None), P(section, dp, None), P())
    return jax.shard_map(body, mesh=fine, in_specs=in_specs, out_specs=out_specs, check_vma=False)
```

```python
import jax
import jax.numpy as jnp
from jax import lax
from jax.experimental import pallas as pl
from jax.experimental.pallas import tpu as pltpu
from jax.sharding import Mesh
from jax.sharding import PartitionSpec as P


HEAD_OUT = 16
TASKS = 6
STEPS = 20
STEP_RATE = 3.0
NX = 4
NC = 2
NY = 4
NZ = 8
SECTIONS = NX * NC
DP = NY * NZ
BF16 = jnp.bfloat16
F32 = jnp.float32


def shift(value, axis, steps):
    count = lax.axis_size(axis)
    return lax.ppermute(value, axis, [(src, (src + steps) % count) for src in range(count)])


def from_later(value, steps):
    return lax.ppermute(value, "x", [(src, src - steps) for src in range(steps, NX)])


def swap_c(value):
    return lax.ppermute(value, "c", [(0, 1), (1, 0)])


def exchange_dp(blocks):
    return lax.all_to_all(blocks, ("y", "z"), 0, 0, tiled=True)


def at(value, index):
    return lax.dynamic_index_in_dim(value, index, 0, keepdims=False)


def rows_at(value, start, size):
    return lax.dynamic_slice_in_dim(value, start, size, 0)


def across(left, right):
    return lax.dot_general(left, right, (((0,), (0,)), ((), ())), preferred_element_type=F32)


VMEM = pl.BlockSpec(memory_space=pltpu.VMEM)
SMEM = pl.BlockSpec(memory_space=pltpu.SMEM)


def local_call(kernel, outs, where, *operands):
    return pl.pallas_call(
        kernel,
        out_shape=tuple(jax.ShapeDtypeStruct(shape, dtype) for shape, dtype in outs),
        in_specs=[SMEM] + [VMEM] * len(operands),
        out_specs=(VMEM,) * len(outs),
    )(where, *operands)


def pack_kernel(
    where_ref, piece_ref, heads_ref, up_ref, own_rep_ref, own_ref, partner_ref,
    got1_ref, got2_ref, got3_ref, sent_ref, factor_ref, rep_ref,
):
    my_x = where_ref[0]
    my_c = where_ref[1]
    my_stage = my_x * NC + my_c
    up_rows = up_ref[...]
    piece = piece_ref[...]
    for d in range(DP):
        sent_ref[d, 0:32, :] = piece
    gots = (None, got1_ref, got2_ref, got3_ref)
    for k in range(NX):
        for r in range(NC):
            stage = ((my_x + k) % NX) * NC + (my_c if r == 0 else 1 - my_c)
            slot = SECTIONS - 1 - stage
            if k == 0:
                rep_rows = own_rep_ref[256 * r : 256 * r + 256, :]
                factor = heads_ref[...] if r == 0 else partner_ref[...]
            else:
                rep_rows = gots[k][256 * r : 256 * r + 256, :]
                factor = gots[k][512 + 256 * r : 768 + 256 * r, :]
            if k or r:
                factor = jnp.where(stage > my_stage, factor, jnp.zeros_like(factor))
            rep_ref[stage] = rep_rows
            factor_ref[slot] = factor
            product = across(factor, up_rows).astype(BF16)
            for i in range(4):
                sent_ref[4 * slot + i, 32:64, :] = product[32 * i : 32 * i + 32]


def heads_kernel(where_ref, got_ref, rep_ref, target_ref, part_ref, cross_ref, head_ref):
    my_stage = where_ref[0] * NC + where_ref[1]
    for z in range(NZ):
        for y in range(NY):
            head_ref[128 * z + 32 * y : 128 * z + 32 * y + 32, :] = got_ref[NZ * y + z, 0:32, :]
    total = None
    square = None
    for z in range(NZ):
        head = head_ref[128 * z : 128 * z + 128, :]
        rep = jnp.concatenate([rep_ref[m, 32 * z : 32 * z + 32, :] for m in range(SECTIONS)], axis=0)
        term = jnp.dot(rep, head, preferred_element_type=F32)
        other = across(head, head)
        total = term if total is None else total + term
        square = other if square is None else square + other
    target = target_ref[...].astype(F32)
    for m in range(SECTIONS):
        rows = total[32 * m : 32 * m + 32]
        part_ref[32 * m : 32 * m + 32, :] = rows - jnp.where(m == my_stage, target, 0.0)
    part_ref[256:384, :] = square
    cross_ref[...] = jnp.sum(got_ref[:, 32:64, :].astype(F32), axis=0).astype(BF16)


def gram_kernel(where_ref, a_ref, b_ref, c_ref, d_ref, mask_ref, cross_ref, sent_ref, residual_ref):
    def value(ref, lo, size):
        return ref[lo : lo + size, :].astype(F32)

    def summed(lo, size):
        pair = value(a_ref, lo, size) + value(c_ref, lo, size)
        return pair + (value(b_ref, lo, size) + value(d_ref, lo, size))

    def squares(ref):
        return value(ref, 256, 128) + value(ref, 384, 128)

    residual = summed(0, 256).astype(BF16)
    residual_ref[...] = residual
    square = (squares(a_ref) + squares(c_ref)) + (squares(b_ref) + squares(d_ref))
    product = square * across(residual, residual)
    mask = mask_ref[...]
    high = lax.Precision.HIGHEST
    half = jnp.dot(mask[0:8], product, precision=high, preferred_element_type=F32)
    part = lax.dot_general(
        half, mask, (((1,), (1,)), ((), ())), precision=high, preferred_element_type=F32
    )
    top = part.astype(BF16)
    tile = jnp.concatenate([part, part - top.astype(F32)], axis=0).astype(BF16)
    cross = cross_ref[...]
    for d in range(DP):
        sent_ref[d, 0:32, :] = cross
        sent_ref[d, 32:48, :] = tile


LATER_ROWS = (1024, 768, 512, 256)
LATER_FROM = (0, 1024, 1792, 2304)
ALL_ROWS = 2560


def chain_kernel(
    where_ref, got_ref, mask_ref, residual_ref, active_ref, own_ref, other_ref,
    slope_own_ref, slope_other_ref,
    keep_ref, send1_ref, send2_ref, send3_ref, inner_ref, mix_ref, middle_ref,
):
    my_x = where_ref[0]
    my_c = where_ref[1]
    my_y = where_ref[2]
    my_stage = my_x * NC + my_c
    tiles = jnp.sum(got_ref[:, 32:48, :].astype(F32), axis=0)
    gram = tiles[0:8] + tiles[8:16]
    rows = lax.broadcasted_iota(jnp.int32, gram.shape, 0)
    lanes = lax.broadcasted_iota(jnp.int32, gram.shape, 1)
    diagonal = jnp.where(rows == lanes, gram, 0.0)
    trace_sum = jnp.sum(jnp.sum(diagonal, axis=1, keepdims=True), axis=0, keepdims=True) + 1e-06
    scaled = gram / trace_sum
    down0 = jnp.where(rows < TASKS, 1.0 / TASKS, 0.0)
    along0 = jnp.where(lanes < TASKS, 1.0 / TASKS, 0.0)

    def advance(counter, carry):
        down, along = carry
        step_down = jnp.sum(scaled * along, axis=1, keepdims=True)
        step_along = jnp.sum(scaled * down, axis=0, keepdims=True)
        total = jnp.sum(down, axis=0, keepdims=True)
        rate = -STEP_RATE / total
        down = down * jnp.exp(rate * step_down)
        along = along * jnp.exp(rate * step_along)
        return down, along

    down, along = lax.fori_loop(0, STEPS, advance, (down0, along0))
    total_along = jnp.sum(along[0:1], axis=1, keepdims=True)
    total_down = jnp.sum(down, axis=0, keepdims=True)
    mix_ref[...] = along / total_along
    column_weight = jnp.sum((down / total_down) * mask_ref[0:8], axis=0, keepdims=True)

    def cross(stage, source):
        away = (stage // NC - my_x) % NX
        start = jnp.where(away == 0, LATER_FROM[0], LATER_FROM[1])
        start = jnp.where(away == 2, LATER_FROM[2], start)
        start = jnp.where(away == 3, LATER_FROM[3], start)
        start = jnp.minimum(start + 128 * (SECTIONS - 1 - source), ALL_ROWS - 128)
        start = pl.multiple_of(start, 128)
        own = own_ref[pl.ds(start, 128), :]
        return jnp.where(my_c == stage % NC, own, other_ref[pl.ds(start, 128), :])

    def slope_of(stage):
        away = (stage // NC - my_x) % NX
        return jnp.where(my_c == stage % NC, slope_own_ref[away], slope_other_ref[away])

    active = active_ref[...]
    weighted = (residual_ref[...].astype(F32) * column_weight).astype(BF16)
    first = across(weighted, active)
    inners = {}
    for stage in range(SECTIONS - 1, -1, -1):
        branch = jnp.dot(weighted, cross(stage, stage), preferred_element_type=F32)
        for s in range(SECTIONS - 1, stage, -1):
            branch = branch + jnp.dot(inners[s], cross(stage, s), preferred_element_type=F32)
        inner = (branch * slope_of(stage).astype(F32)).astype(BF16)
        inners[stage] = inner

        @pl.when(stage == my_stage)
        def _():
            inner_ref[...] = inner
            send1_ref[256:512, :] = inner
            send2_ref[256:512, :] = inner
            send3_ref[256:512, :] = inner

        product = jnp.where(stage > my_stage, across(inner, active), 0.0)
        product = jnp.where(stage == my_stage, first, product)
        lo = 128 * (SECTIONS - 1 - stage)
        middle_ref[lo : lo + 128, :] = product.astype(BF16)

    for k, ref in enumerate((keep_ref, send1_ref, send2_ref, send3_ref)):
        start = pl.multiple_of(((my_y - k) % NY) * 256, 256)
        ref[0:256, :] = middle_ref[pl.ds(start, 256), :]


def down_kernel(
    y_ref, x0_ref, x1_ref, x2a_ref, x2b_ref, x3_ref, inner_ref, keep_ref, got1_ref, got2_ref, got3_ref,
    out_ref,
):
    step = pl.program_id(0)
    x2 = jnp.where(step < 2, x2a_ref[...], x2b_ref[...])
    total = across(inner_ref[...], x0_ref[...])
    total = total + across(got1_ref[256:512, :], x1_ref[...])
    total = total + across(got2_ref[256:512, :], x2)
    total = total + across(got3_ref[256:512, :], x3_ref[...])
    total = total.astype(BF16)
    for j in range(2):
        for h in range(2):
            lo = 256 * j + 128 * h
            out_ref[j, 128 * h : 128 * h + 128, :] = total[:, lo : lo + 128]
        start = pl.multiple_of((2 * step + j) * 32, 32)
        rows = [ref[pl.ds(start, 32), :].astype(F32) for ref in (keep_ref, got1_ref, got2_ref, got3_ref)]
        out_ref[j, 256:288, :] = ((rows[0] + rows[1]) + (rows[2] + rows[3])).astype(BF16)


def run_down(my_y, saved, x1, x2a, x2b, x3, inner, keep, got1, got2, got3):
    cols = 512
    whole = lambda value: pl.BlockSpec(value.shape, lambda i, y: (0, 0))
    block = (256, cols)
    return pl.pallas_call(
        down_kernel,
        grid_spec=pltpu.PrefetchScalarGridSpec(
            num_scalar_prefetch=1,
            grid=(4,),
            in_specs=[
                pl.BlockSpec(block, lambda i, y: (0, 4 * y[0] + i)),
                pl.BlockSpec(block, lambda i, y: (0, i)),
                pl.BlockSpec(block, lambda i, y: (0, jnp.minimum(i, 1))),
                pl.BlockSpec(block, lambda i, y: (0, jnp.maximum(i - 2, 0))),
                pl.BlockSpec(block, lambda i, y: (0, i)),
                whole(inner), whole(keep), whole(got1), whole(got2), whole(got3),
            ],
            out_specs=pl.BlockSpec((2, 288, 128), lambda i, y: (i, 0, 0)),
        ),
        out_shape=jax.ShapeDtypeStruct((NZ, 288, 128), BF16),
        name="down_product",
    )(my_y.reshape(1), saved, x1, x2a, x2b, x3, inner, keep, got1, got2, got3)


def stages(
    section_inputs, adapter_down, adapter_up, representation, head_weights, head_targets, head_task
):
    my_x = lax.axis_index("x")
    my_c = lax.axis_index("c")
    my_y = lax.axis_index("y")
    my_dp = my_y * NZ + lax.axis_index("z")
    where = jnp.stack([my_x, my_c, my_y]).astype(jnp.int32)
    dim_model = section_inputs.shape[3]
    saved = section_inputs[0].reshape(-1, dim_model)
    down_map = adapter_down[0]
    up_map = adapter_up[0]
    heads = head_weights
    share, rank = heads.shape
    tok = representation.shape[1]
    column_task = jnp.repeat(head_task[:, 0], HEAD_OUT)
    mask = (column_task[None, :] == jnp.arange(rank, dtype=jnp.int32)[:, None]).astype(F32)

    piece = rows_at(heads, my_c * 128 + my_x * 32, 32)
    turn = [(a * NY + b, b * NY + a) for a in range(NX) for b in range(NY)]
    piece = lax.ppermute(piece, ("x", "y"), turn)

    blocks = representation[0].reshape(tok, NX, NZ, NC, 128).transpose(3, 1, 2, 0, 4)
    blocks = blocks.reshape(NC, NX, NZ * tok, 128)
    down_rows = rows_at(down_map, my_dp * share, share)
    swapped = swap_c(at(blocks, 1 - my_c))
    partner = swap_c(down_rows)
    pair = jnp.concatenate([at(blocks, my_c), swapped], axis=1)
    gots = []
    for k in range(1, NX):
        sent = jnp.concatenate([at(pair, (my_x - k) % NX), down_rows, partner], axis=0)
        gots.append(shift(sent, "x", -k))

    wide = dim_model // NY

    def cut(index, k, lo, size):
        return lax.dynamic_slice_in_dim(saved, ((index - k) % NY) * wide + lo, size, 1)

    x1 = shift(cut(my_y, 1, 0, wide), "y", -1)
    x3 = shift(cut(my_y, 3, 0, wide), "y", -3)

    up_rows = rows_at(up_map, my_dp * share, share)
    sent, factors, rep = local_call(
        pack_kernel,
        [((DP, 64, rank), BF16), ((SECTIONS, share, rank), BF16), ((SECTIONS, NZ * tok, rank), BF16)],
        where, piece, heads, up_rows, at(pair, my_x), down_rows, partner, *gots,
    )

    preact = jnp.dot(saved, down_map, preferred_element_type=F32)
    logistic = jax.nn.sigmoid(preact)
    active = (preact * logistic).astype(BF16)
    slope = (logistic * (1.0 + preact * (1.0 - logistic))).astype(BF16)
    slope_own = jnp.stack([slope] + [from_later(slope, k) for k in range(1, NX)])
    slope_other = swap_c(slope_own)

    got = exchange_dp(sent)
    part, cross_rows, _ = local_call(
        heads_kernel,
        [((384, rank), F32), ((32, rank), BF16), ((1024, rank), BF16)],
        where, got, rep, head_targets[0],
    )
    part = part + swap_c(part)
    top = part.astype(BF16)
    low = (part[256:] - top[256:].astype(F32)).astype(BF16)
    halves = jnp.concatenate([top, low], axis=0)
    others = [shift(halves, "x", -k) for k in range(1, NX)]
    x2a = shift(cut(my_y, 2, 0, wide // 2), "y", -2)
    sent, residual = local_call(
        gram_kernel,
        [((DP, 48, rank), BF16), ((256, rank), BF16)],
        where, halves, *others, mask, cross_rows,
    )
    got = exchange_dp(sent)
    cross = got[:, :32].reshape(-1, rank)
    kept = [cross]
    for k in range(1, NX):
        kept.append(from_later(cross[: LATER_ROWS[k]], k))
    x2b = shift(cut(my_y, 2, wide // 2, wide // 2), "y", -2)
    cross_own = jnp.concatenate(kept, axis=0)
    cross_other = swap_c(cross_own)
    keep, send1, send2, send3, inner, mix, _ = local_call(
        chain_kernel,
        [((256, rank), BF16)] + [((512, rank), BF16)] * 3
        + [((256, rank), BF16), ((8, rank), F32), ((1024, rank), BF16)],
        where, got, mask, residual, active, cross_own, cross_other, slope_own, slope_other,
    )
    got1 = shift(send1, "y", -1)
    got2 = shift(send2, "y", -2)
    got3 = shift(send3, "y", -3)
    part_down = run_down(my_y, saved, x1, x2a, x2b, x3, inner, keep, got1, got2, got3)
    got = lax.all_to_all(part_down, "z", 0, 0, tiled=True)
    total = jnp.sum(got.astype(F32), axis=0)
    rows = total[256:].astype(BF16)
    middle = exchange_dp(jnp.broadcast_to(rows[None], (DP, 32, rank)))
    middle = middle.reshape(SECTIONS, rank, rank)
    grad_up = lax.dot_general(
        factors, middle, (((0, 2), (0, 1)), ((), ())), preferred_element_type=F32
    )
    grad_down = jnp.concatenate([total[:128].T, total[128:256].T], axis=0)
    return (grad_down[None], grad_up[None], mix[0, :TASKS])


def solution(mesh):
    fine = Mesh(mesh.devices.reshape(NX, NC, NY, NZ), ("x", "c", "y", "z"))
    section = ("x", "c")
    dp = ("y", "z")
    in_specs = (
        P(section, None, dp, None),
        P(section, None, None),
        P(section, None, None),
        P(section, dp, None),
        P(dp, None),
        P(section, dp, None),
        P(),
    )
    out_specs = (P(section, dp, None), P(section, dp, None), P())
    return jax.shard_map(stages, mesh=fine, in_specs=in_specs, out_specs=out_specs, check_vma=False)
```

```python
import jax
import jax.numpy as jnp
from jax import lax
from jax.experimental import pallas as pl
from jax.experimental.pallas import tpu as pltpu
from jax.sharding import Mesh
from jax.sharding import PartitionSpec as P


HEAD_OUT = 16
TASKS = 6
STEPS = 20
STEP_RATE = 3.0
NX = 4
NC = 2
NY = 4
NZ = 8
SECTIONS = NX * NC
DP = NY * NZ
BF16 = jnp.bfloat16
F32 = jnp.float32


def shift(value, axis, steps):
    count = lax.axis_size(axis)
    return lax.ppermute(value, axis, [(src, (src + steps) % count) for src in range(count)])


def from_later(value, steps):
    return lax.ppermute(value, "x", [(src, src - steps) for src in range(steps, NX)])


def swap_c(value):
    return lax.ppermute(value, "c", [(0, 1), (1, 0)])


def exchange_dp(blocks):
    return lax.all_to_all(blocks, ("y", "z"), 0, 0, tiled=True)


def rows_at(value, start, size):
    return lax.dynamic_slice_in_dim(value, start, size, 0)


def across(left, right):
    return lax.dot_general(left, right, (((0,), (0,)), ((), ())), preferred_element_type=F32)


VMEM = pl.BlockSpec(memory_space=pltpu.VMEM)
SMEM = pl.BlockSpec(memory_space=pltpu.SMEM)


def local_call(kernel, outs, where, *operands):
    return pl.pallas_call(
        kernel,
        out_shape=tuple(jax.ShapeDtypeStruct(shape, dtype) for shape, dtype in outs),
        in_specs=[SMEM] + [VMEM] * len(operands),
        out_specs=(VMEM,) * len(outs),
    )(where, *operands)


def pack_kernel(
    where_ref, heads_ref, up_ref, own_ref, partner_ref, got1_ref, got2_ref, got3_ref,
    sent_ref, factor_ref,
):
    my_x = where_ref[0]
    my_c = where_ref[1]
    my_stage = my_x * NC + my_c
    up_rows = up_ref[...]
    gots = (None, got1_ref, got2_ref, got3_ref)
    for k in range(NX):
        for r in range(NC):
            stage = ((my_x + k) % NX) * NC + (my_c if r == 0 else 1 - my_c)
            slot = SECTIONS - 1 - stage
            if k == 0:
                factor = heads_ref[...] if r == 0 else partner_ref[...]
            else:
                factor = gots[k][256 * r : 256 * r + 256, :]
            if k or r:
                factor = jnp.where(stage > my_stage, factor, jnp.zeros_like(factor))
            factor_ref[slot] = factor
            product = across(factor, up_rows).astype(BF16)
            for i in range(4):
                sent_ref[4 * slot + i] = product[32 * i : 32 * i + 32]


def assemble_kernel(where_ref, own_ref, other_ref, out_ref):
    my_x = where_ref[0]
    my_c = where_ref[1]
    for k in range(NX):
        base = ((my_x + k) % NX) * NC
        out_ref[:, base + my_c] = own_ref[k]
        out_ref[:, base + 1 - my_c] = other_ref[k]


def gram_kernel(where_ref, residual_ref, square_ref, mask_ref, cross_ref, sent_ref):
    residual = residual_ref[...]
    product = square_ref[...] * across(residual, residual)
    mask = mask_ref[...]
    high = lax.Precision.HIGHEST
    half = jnp.dot(mask[0:8], product, precision=high, preferred_element_type=F32)
    part = lax.dot_general(
        half, mask, (((1,), (1,)), ((), ())), precision=high, preferred_element_type=F32
    )
    top = part.astype(BF16)
    tile = jnp.concatenate([part, part - top.astype(F32)], axis=0).astype(BF16)
    cross = jnp.sum(cross_ref[...].astype(F32), axis=0).astype(BF16)
    for d in range(DP):
        sent_ref[d, 0:32, :] = cross
        sent_ref[d, 32:48, :] = tile


def merge_kernel(where_ref, residual_ref, got_ref, out_ref):
    out_ref[0:32, :] = residual_ref[...]
    tile = jnp.sum(got_ref[:, 32:48, :].astype(F32), axis=0)
    part = tile[0:8] + tile[8:16]
    top = part.astype(BF16).astype(F32)
    out_ref[32:48, :] = jnp.concatenate([part, part - top], axis=0).astype(BF16)
    for d in range(DP):
        out_ref[48 + 32 * d : 80 + 32 * d, :] = got_ref[d, 0:32, :]


SMALL = 48
LATER_ROWS = (1024, 768, 512, 256)
LATER_FROM = (0, 1072, 1888, 2448)
ALL_ROWS = 2752


def chain_kernel(
    where_ref, mask_ref, active_ref, own_ref, other_ref, slope_own_ref, slope_other_ref,
    keep_ref, send1_ref, send2_ref, send3_ref, inner_ref, mix_ref, middle_ref,
):
    my_x = where_ref[0]
    my_c = where_ref[1]
    my_y = where_ref[2]
    my_stage = my_x * NC + my_c
    tiles = []
    for k in range(NX):
        lo = LATER_FROM[k] + 32
        tiles.append(own_ref[lo : lo + 16, :].astype(F32) + other_ref[lo : lo + 16, :].astype(F32))
    tile = (tiles[0] + tiles[2]) + (tiles[1] + tiles[3])
    gram = tile[0:8] + tile[8:16]
    rows = lax.broadcasted_iota(jnp.int32, gram.shape, 0)
    lanes = lax.broadcasted_iota(jnp.int32, gram.shape, 1)
    diagonal = jnp.where(rows == lanes, gram, 0.0)
    trace_sum = jnp.sum(jnp.sum(diagonal, axis=1, keepdims=True), axis=0, keepdims=True) + 1e-06
    scaled = gram / trace_sum
    down0 = jnp.where(rows < TASKS, 1.0 / TASKS, 0.0)
    along0 = jnp.where(lanes < TASKS, 1.0 / TASKS, 0.0)

    def advance(counter, carry):
        down, along = carry
        step_down = jnp.sum(scaled * along, axis=1, keepdims=True)
        step_along = jnp.sum(scaled * down, axis=0, keepdims=True)
        total = jnp.sum(down, axis=0, keepdims=True)
        rate = -STEP_RATE / total
        down = down * jnp.exp(rate * step_down)
        along = along * jnp.exp(rate * step_along)
        return down, along

    down, along = lax.fori_loop(0, STEPS, advance, (down0, along0))
    total_along = jnp.sum(along[0:1], axis=1, keepdims=True)
    total_down = jnp.sum(down, axis=0, keepdims=True)
    mix_ref[...] = along / total_along
    column_weight = jnp.sum((down / total_down) * mask_ref[0:8], axis=0, keepdims=True)

    def first_row(stage):
        away = (stage // NC - my_x) % NX
        start = jnp.where(away == 0, LATER_FROM[0], LATER_FROM[1])
        start = jnp.where(away == 2, LATER_FROM[2], start)
        return jnp.where(away == 3, LATER_FROM[3], start)

    def taken(stage, start, size):
        start = pl.multiple_of(start, 16)
        own = own_ref[pl.ds(start, size), :]
        return jnp.where(my_c == stage % NC, own, other_ref[pl.ds(start, size), :])

    def cross(stage, source):
        start = first_row(stage) + SMALL + 128 * (SECTIONS - 1 - source)
        return taken(stage, jnp.minimum(start, ALL_ROWS - 128), 128)

    def slope_of(stage):
        away = (stage // NC - my_x) % NX
        return jnp.where(my_c == stage % NC, slope_own_ref[away], slope_other_ref[away])

    active = active_ref[...]
    residual = jnp.concatenate([taken(m, first_row(m), 32) for m in range(SECTIONS)], axis=0)
    weighted = (residual.astype(F32) * column_weight).astype(BF16)
    first = across(weighted, active)
    inners = {}
    for stage in range(SECTIONS - 1, -1, -1):
        branch = jnp.dot(weighted, cross(stage, stage), preferred_element_type=F32)
        for s in range(SECTIONS - 1, stage, -1):
            branch = branch + jnp.dot(inners[s], cross(stage, s), preferred_element_type=F32)
        inner = (branch * slope_of(stage).astype(F32)).astype(BF16)
        inners[stage] = inner

        @pl.when(stage == my_stage)
        def _():
            inner_ref[...] = inner
            send1_ref[256:512, :] = inner
            send2_ref[256:512, :] = inner
            send3_ref[256:512, :] = inner

        product = jnp.where(stage > my_stage, across(inner, active), 0.0)
        product = jnp.where(stage == my_stage, first, product)
        lo = 128 * (SECTIONS - 1 - stage)
        middle_ref[lo : lo + 128, :] = product.astype(BF16)

    for k, ref in enumerate((keep_ref, send1_ref, send2_ref, send3_ref)):
        start = pl.multiple_of(((my_y - k) % NY) * 256, 256)
        ref[0:256, :] = middle_ref[pl.ds(start, 256), :]


def down_kernel(
    y_ref, x0_ref, x1_ref, x2a_ref, x2b_ref, x3_ref, inner_ref, keep_ref, got1_ref, got2_ref, got3_ref,
    out_ref,
):
    step = pl.program_id(0)
    x2 = jnp.where(step < 2, x2a_ref[...], x2b_ref[...])
    total = across(inner_ref[...], x0_ref[...])
    total = total + across(got1_ref[256:512, :], x1_ref[...])
    total = total + across(got2_ref[256:512, :], x2)
    total = total + across(got3_ref[256:512, :], x3_ref[...])
    total = total.astype(BF16)
    for j in range(2):
        for h in range(2):
            lo = 256 * j + 128 * h
            out_ref[j, 128 * h : 128 * h + 128, :] = total[:, lo : lo + 128]
        start = pl.multiple_of((2 * step + j) * 32, 32)
        rows = [ref[pl.ds(start, 32), :].astype(F32) for ref in (keep_ref, got1_ref, got2_ref, got3_ref)]
        out_ref[j, 256:288, :] = ((rows[0] + rows[1]) + (rows[2] + rows[3])).astype(BF16)


def run_down(my_y, saved, x1, x2a, x2b, x3, inner, keep, got1, got2, got3):
    cols = 512
    whole = lambda value: pl.BlockSpec(value.shape, lambda i, y: (0, 0))
    block = (256, cols)
    return pl.pallas_call(
        down_kernel,
        grid_spec=pltpu.PrefetchScalarGridSpec(
            num_scalar_prefetch=1,
            grid=(4,),
            in_specs=[
                pl.BlockSpec(block, lambda i, y: (0, 4 * y[0] + i)),
                pl.BlockSpec(block, lambda i, y: (0, i)),
                pl.BlockSpec(block, lambda i, y: (0, jnp.minimum(i, 1))),
                pl.BlockSpec(block, lambda i, y: (0, jnp.maximum(i - 2, 0))),
                pl.BlockSpec(block, lambda i, y: (0, i)),
                whole(inner), whole(keep), whole(got1), whole(got2), whole(got3),
            ],
            out_specs=pl.BlockSpec((2, 288, 128), lambda i, y: (i, 0, 0)),
        ),
        out_shape=jax.ShapeDtypeStruct((NZ, 288, 128), BF16),
        name="down_product",
    )(my_y.reshape(1), saved, x1, x2a, x2b, x3, inner, keep, got1, got2, got3)


def stages(
    section_inputs, adapter_down, adapter_up, representation, head_weights, head_targets, head_task
):
    my_x = lax.axis_index("x")
    my_c = lax.axis_index("c")
    my_y = lax.axis_index("y")
    my_dp = my_y * NZ + lax.axis_index("z")
    where = jnp.stack([my_x, my_c, my_y]).astype(jnp.int32)
    dim_model = section_inputs.shape[3]
    saved = section_inputs[0].reshape(-1, dim_model)
    down_map = adapter_down[0]
    up_map = adapter_up[0]
    heads = head_weights
    share, rank = heads.shape
    column_task = jnp.repeat(head_task[:, 0], HEAD_OUT)
    mask = (column_task[None, :] == jnp.arange(rank, dtype=jnp.int32)[:, None]).astype(F32)

    down_rows = rows_at(down_map, my_dp * share, share)
    partner = swap_c(down_rows)
    both = jnp.concatenate([down_rows, partner], axis=0)
    gots = [from_later(both, k) for k in range(1, NX)]

    piece = rows_at(heads, my_x * 64 + my_c * 32, 32)
    pieces = exchange_dp(jnp.broadcast_to(piece[None], (DP, 32, rank)))
    near = [pieces]
    for k in range(1, NX):
        near.append(shift(pieces, "x", -k))

    wide = dim_model // NY

    def cut(index, k, lo, size):
        return lax.dynamic_slice_in_dim(saved, ((index - k) % NY) * wide + lo, size, 1)

    x1 = shift(cut(my_y, 1, 0, wide), "y", -1)
    x3 = shift(cut(my_y, 3, 0, wide), "y", -3)

    up_rows = rows_at(up_map, my_dp * share, share)
    sent, factors = local_call(
        pack_kernel,
        [((DP, 32, rank), BF16), ((SECTIONS, share, rank), BF16)],
        where, heads, up_rows, down_rows, partner, *gots,
    )
    down_late, sent = lax.optimization_barrier((down_map, sent))
    got_cross = exchange_dp(sent)

    preact = jnp.dot(saved, down_late, preferred_element_type=F32)
    logistic = jax.nn.sigmoid(preact)
    active = (preact * logistic).astype(BF16)
    slope = (logistic * (1.0 + preact * (1.0 - logistic))).astype(BF16)
    slope_own = jnp.stack([slope] + [from_later(slope, k) for k in range(1, NX)])
    slope_other = swap_c(slope_own)

    near, got_cross = lax.optimization_barrier((jnp.stack(near), got_cross))
    far = swap_c(near)
    (weights,) = local_call(assemble_kernel, [((DP, SECTIONS, 32, rank), BF16)], where, near, far)
    weights = weights.reshape(dim_model, rank)
    predicted = jnp.dot(representation[0], weights, preferred_element_type=F32)
    residual = (predicted - head_targets[0].astype(F32)).astype(BF16)
    x2a = shift(cut(my_y, 2, 0, wide // 2), "y", -2)
    (sent,) = local_call(
        gram_kernel, [((DP, SMALL, rank), BF16)],
        where, residual, across(weights, weights), mask, got_cross,
    )
    got = exchange_dp(sent)
    (cross,) = local_call(merge_kernel, [((SMALL + 1024, rank), BF16)], where, residual, got)
    kept = [cross]
    for k in range(1, NX):
        kept.append(shift(cross[: SMALL + LATER_ROWS[k]], "x", -k))
    x2b = shift(cut(my_y, 2, wide // 2, wide // 2), "y", -2)
    cross_own = jnp.concatenate(kept, axis=0)
    cross_other = swap_c(cross_own)
    keep, send1, send2, send3, inner, mix, _ = local_call(
        chain_kernel,
        [((256, rank), BF16)] + [((512, rank), BF16)] * 3
        + [((256, rank), BF16), ((8, rank), F32), ((1024, rank), BF16)],
        where, mask, active, cross_own, cross_other, slope_own, slope_other,
    )
    got1 = shift(send1, "y", -1)
    got2 = shift(send2, "y", -2)
    got3 = shift(send3, "y", -3)
    part_down = run_down(my_y, saved, x1, x2a, x2b, x3, inner, keep, got1, got2, got3)
    got = lax.all_to_all(part_down, "z", 0, 0, tiled=True)
    total = jnp.sum(got.astype(F32), axis=0)
    rows = total[256:].astype(BF16)
    middle = exchange_dp(jnp.broadcast_to(rows[None], (DP, 32, rank)))
    middle = middle.reshape(SECTIONS, rank, rank)
    grad_up = lax.dot_general(
        factors, middle, (((0, 2), (0, 1)), ((), ())), preferred_element_type=F32
    )
    grad_down = jnp.concatenate([total[:128].T, total[128:256].T], axis=0)
    return (grad_down[None], grad_up[None], mix[0, :TASKS])


def solution(mesh):
    fine = Mesh(mesh.devices.reshape(NX, NC, NY, NZ), ("x", "c", "y", "z"))
    section = ("x", "c")
    dp = ("y", "z")
    in_specs = (
        P(section, None, dp, None),
        P(section, None, None),
        P(section, None, None),
        P(section, dp, None),
        P(dp, None),
        P(section, dp, None),
        P(),
    )
    out_specs = (P(section, dp, None), P(section, dp, None), P())
    return jax.shard_map(stages, mesh=fine, in_specs=in_specs, out_specs=out_specs, check_vma=False)
```

```python
import jax
import jax.numpy as jnp
from jax import lax
from jax.experimental import pallas as pl
from jax.experimental.pallas import tpu as pltpu
from jax.sharding import Mesh
from jax.sharding import PartitionSpec as P


HEAD_OUT = 16
TASKS = 6
STEPS = 20
STEP_RATE = 3.0
NX = 4
NC = 2
NY = 4
NZ = 8
SECTIONS = NX * NC
DP = NY * NZ
BF16 = jnp.bfloat16
F32 = jnp.float32


def shift(value, axis, steps):
    count = lax.axis_size(axis)
    return lax.ppermute(value, axis, [(src, (src + steps) % count) for src in range(count)])


def from_later(value, steps):
    return lax.ppermute(value, "x", [(src, src - steps) for src in range(steps, NX)])


def swap_c(value):
    return lax.ppermute(value, "c", [(0, 1), (1, 0)])


def exchange_dp(blocks):
    return lax.all_to_all(blocks, ("y", "z"), 0, 0, tiled=True)


def at(value, index):
    return lax.dynamic_index_in_dim(value, index, 0, keepdims=False)


def rows_at(value, start, size):
    return lax.dynamic_slice_in_dim(value, start, size, 0)


def across(left, right):
    return lax.dot_general(left, right, (((0,), (0,)), ((), ())), preferred_element_type=F32)


VMEM = pl.BlockSpec(memory_space=pltpu.VMEM)
SMEM = pl.BlockSpec(memory_space=pltpu.SMEM)


def local_call(kernel, outs, where, *operands):
    return pl.pallas_call(
        kernel,
        out_shape=tuple(jax.ShapeDtypeStruct(shape, dtype) for shape, dtype in outs),
        in_specs=[SMEM] + [VMEM] * len(operands),
        out_specs=(VMEM,) * len(outs),
    )(where, *operands)


def pack_kernel(
    where_ref, piece_ref, heads_ref, up_ref, own_rep_ref, own_ref, partner_ref,
    got1_ref, got2_ref, got3_ref, sent_ref, factor_ref, rep_ref,
):
    my_x = where_ref[0]
    my_c = where_ref[1]
    my_stage = my_x * NC + my_c
    up_rows = up_ref[...]
    piece = piece_ref[...]
    for d in range(DP):
        sent_ref[d, 0:32, :] = piece
    gots = (None, got1_ref, got2_ref, got3_ref)
    for k in range(NX):
        for r in range(NC):
            stage = ((my_x + k) % NX) * NC + (my_c if r == 0 else 1 - my_c)
            slot = SECTIONS - 1 - stage
            if k == 0:
                rep_rows = own_rep_ref[256 * r : 256 * r + 256, :]
                factor = heads_ref[...] if r == 0 else partner_ref[...]
            else:
                rep_rows = gots[k][256 * r : 256 * r + 256, :]
                factor = gots[k][512 + 256 * r : 768 + 256 * r, :]
            if k or r:
                factor = jnp.where(stage > my_stage, factor, jnp.zeros_like(factor))
            rep_ref[stage] = rep_rows
            factor_ref[slot] = factor
            product = across(factor, up_rows).astype(BF16)
            for i in range(4):
                sent_ref[4 * slot + i, 32:64, :] = product[32 * i : 32 * i + 32]


def heads_kernel(where_ref, got_ref, rep_ref, target_ref, part_ref, cross_ref, head_ref):
    my_stage = where_ref[0] * NC + where_ref[1]
    for z in range(NZ):
        for y in range(NY):
            head_ref[128 * z + 32 * y : 128 * z + 32 * y + 32, :] = got_ref[NZ * y + z, 0:32, :]
    total = None
    square = None
    for z in range(NZ):
        head = head_ref[128 * z : 128 * z + 128, :]
        rep = jnp.concatenate([rep_ref[m, 32 * z : 32 * z + 32, :] for m in range(SECTIONS)], axis=0)
        term = jnp.dot(rep, head, preferred_element_type=F32)
        other = across(head, head)
        total = term if total is None else total + term
        square = other if square is None else square + other
    target = target_ref[...].astype(F32)
    for m in range(SECTIONS):
        rows = total[32 * m : 32 * m + 32]
        part_ref[32 * m : 32 * m + 32, :] = rows - jnp.where(m == my_stage, target, 0.0)
    part_ref[256:384, :] = square
    cross_ref[...] = jnp.sum(got_ref[:, 32:64, :].astype(F32), axis=0).astype(BF16)


def gram_kernel(where_ref, a_ref, b_ref, c_ref, d_ref, mask_ref, cross_ref, sent_ref, residual_ref):
    def value(ref, lo, size):
        return ref[lo : lo + size, :].astype(F32)

    def summed(lo, size):
        pair = value(a_ref, lo, size) + value(c_ref, lo, size)
        return pair + (value(b_ref, lo, size) + value(d_ref, lo, size))

    def squares(ref):
        return value(ref, 256, 128) + value(ref, 384, 128)

    residual = summed(0, 256).astype(BF16)
    residual_ref[...] = residual
    square = (squares(a_ref) + squares(c_ref)) + (squares(b_ref) + squares(d_ref))
    product = square * across(residual, residual)
    mask = mask_ref[...]
    high = lax.Precision.HIGHEST
    half = jnp.dot(mask[0:8], product, precision=high, preferred_element_type=F32)
    part = lax.dot_general(
        half, mask, (((1,), (1,)), ((), ())), precision=high, preferred_element_type=F32
    )
    top = part.astype(BF16)
    tile = jnp.concatenate([part, part - top.astype(F32)], axis=0).astype(BF16)
    cross = cross_ref[...]
    for d in range(DP):
        sent_ref[d, 0:32, :] = cross
        sent_ref[d, 32:48, :] = tile


LATER_ROWS = (1024, 768, 512, 256)
LATER_FROM = (0, 1024, 1792, 2304)
ALL_ROWS = 2560


def chain_kernel(
    where_ref, got_ref, mask_ref, residual_ref, active_ref, own_ref, other_ref,
    slope_own_ref, slope_other_ref,
    keep_ref, send1_ref, send2_ref, send3_ref, inner_ref, mix_ref, middle_ref,
):
    my_x = where_ref[0]
    my_c = where_ref[1]
    my_y = where_ref[2]
    my_stage = my_x * NC + my_c
    tiles = jnp.sum(got_ref[:, 32:48, :].astype(F32), axis=0)
    gram = tiles[0:8] + tiles[8:16]
    rows = lax.broadcasted_iota(jnp.int32, gram.shape, 0)
    lanes = lax.broadcasted_iota(jnp.int32, gram.shape, 1)
    diagonal = jnp.where(rows == lanes, gram, 0.0)
    trace_sum = jnp.sum(jnp.sum(diagonal, axis=1, keepdims=True), axis=0, keepdims=True) + 1e-06
    scaled = gram * (-STEP_RATE / trace_sum)
    tasks = range(TASKS)
    entry = [[jnp.broadcast_to(scaled[t : t + 1, u : u + 1], (8, 128)) for u in tasks] for t in tasks]

    def advance(counter, weights):
        total = ((weights[0] + weights[1]) + (weights[2] + weights[3])) + (weights[4] + weights[5])
        inverse = 1.0 / total
        moved = []
        for t in tasks:
            terms = [entry[t][u] * weights[u] for u in tasks]
            step = ((terms[0] + terms[1]) + (terms[2] + terms[3])) + (terms[4] + terms[5])
            moved.append(weights[t] * jnp.exp(step * inverse))
        return tuple(moved)

    even = jnp.full((8, 128), 1.0 / TASKS, F32)
    weights = lax.fori_loop(0, STEPS, advance, (even,) * TASKS)
    total = ((weights[0] + weights[1]) + (weights[2] + weights[3])) + (weights[4] + weights[5])
    weights = [weight / total for weight in weights]
    mix = jnp.zeros((8, 128), F32)
    column_weight = jnp.zeros((1, 128), F32)
    for t in tasks:
        mix = jnp.where(lanes == t, weights[t], mix)
        column_weight = column_weight + weights[t][0:1] * mask_ref[t : t + 1]
    mix_ref[...] = mix

    def cross(stage, source):
        away = (stage // NC - my_x) % NX
        start = jnp.where(away == 0, LATER_FROM[0], LATER_FROM[1])
        start = jnp.where(away == 2, LATER_FROM[2], start)
        start = jnp.where(away == 3, LATER_FROM[3], start)
        start = jnp.minimum(start + 128 * (SECTIONS - 1 - source), ALL_ROWS - 128)
        start = pl.multiple_of(start, 128)
        own = own_ref[pl.ds(start, 128), :]
        return jnp.where(my_c == stage % NC, own, other_ref[pl.ds(start, 128), :])

    def slope_of(stage):
        away = (stage // NC - my_x) % NX
        return jnp.where(my_c == stage % NC, slope_own_ref[away], slope_other_ref[away])

    active = active_ref[...].T
    weighted = (residual_ref[...].astype(F32) * column_weight).astype(BF16)
    first = jnp.dot(active, weighted, preferred_element_type=F32)
    inners = {}
    for stage in range(SECTIONS - 1, -1, -1):
        left = [weighted] + [inners[s] for s in range(SECTIONS - 1, stage, -1)]
        right = [cross(stage, s) for s in [stage] + list(range(SECTIONS - 1, stage, -1))]
        branch = None
        for n in range(0, len(left), 2):
            term = jnp.dot(
                jnp.concatenate(left[n : n + 2], axis=1),
                jnp.concatenate(right[n : n + 2], axis=0),
                preferred_element_type=F32,
            )
            branch = term if branch is None else branch + term
        inner = (branch * slope_of(stage).astype(F32)).astype(BF16)
        inners[stage] = inner

        @pl.when(stage == my_stage)
        def _():
            inner_ref[...] = inner
            send1_ref[256:512, :] = inner
            send2_ref[256:512, :] = inner
            send3_ref[256:512, :] = inner

        product = jnp.dot(active, inner, preferred_element_type=F32)
        product = jnp.where(stage > my_stage, product, 0.0)
        product = jnp.where(stage == my_stage, first, product)
        lo = 128 * (SECTIONS - 1 - stage)
        middle_ref[lo : lo + 128, :] = product.astype(BF16)

    for k, ref in enumerate((keep_ref, send1_ref, send2_ref, send3_ref)):
        start = pl.multiple_of(((my_y - k) % NY) * 256, 256)
        ref[0:256, :] = middle_ref[pl.ds(start, 256), :]


def down_kernel(
    y_ref, x0_ref, x1_ref, x2a_ref, x2b_ref, x3_ref, inner_ref, keep_ref, got1_ref, got2_ref, got3_ref,
    out_ref,
):
    step = pl.program_id(0)
    x2 = jnp.where(step < 2, x2a_ref[...], x2b_ref[...])
    total = across(inner_ref[...], x0_ref[...])
    total = total + across(got1_ref[256:512, :], x1_ref[...])
    total = total + across(got2_ref[256:512, :], x2)
    total = total + across(got3_ref[256:512, :], x3_ref[...])
    total = total.astype(BF16)
    for j in range(2):
        for h in range(2):
            lo = 256 * j + 128 * h
            out_ref[j, 128 * h : 128 * h + 128, :] = total[:, lo : lo + 128]
        start = pl.multiple_of((2 * step + j) * 32, 32)
        rows = [ref[pl.ds(start, 32), :].astype(F32) for ref in (keep_ref, got1_ref, got2_ref, got3_ref)]
        out_ref[j, 256:288, :] = ((rows[0] + rows[1]) + (rows[2] + rows[3])).astype(BF16)


def run_down(my_y, saved, x1, x2a, x2b, x3, inner, keep, got1, got2, got3):
    cols = 512
    whole = lambda value: pl.BlockSpec(value.shape, lambda i, y: (0, 0))
    block = (256, cols)
    return pl.pallas_call(
        down_kernel,
        grid_spec=pltpu.PrefetchScalarGridSpec(
            num_scalar_prefetch=1,
            grid=(4,),
            in_specs=[
                pl.BlockSpec(block, lambda i, y: (0, 4 * y[0] + i)),
                pl.BlockSpec(block, lambda i, y: (0, i)),
                pl.BlockSpec(block, lambda i, y: (0, jnp.minimum(i, 1))),
                pl.BlockSpec(block, lambda i, y: (0, jnp.maximum(i - 2, 0))),
                pl.BlockSpec(block, lambda i, y: (0, i)),
                whole(inner), whole(keep), whole(got1), whole(got2), whole(got3),
            ],
            out_specs=pl.BlockSpec((2, 288, 128), lambda i, y: (i, 0, 0)),
        ),
        out_shape=jax.ShapeDtypeStruct((NZ, 288, 128), BF16),
        name="down_product",
    )(my_y.reshape(1), saved, x1, x2a, x2b, x3, inner, keep, got1, got2, got3)


def stages(
    section_inputs, adapter_down, adapter_up, representation, head_weights, head_targets, head_task
):
    my_x = lax.axis_index("x")
    my_c = lax.axis_index("c")
    my_y = lax.axis_index("y")
    my_dp = my_y * NZ + lax.axis_index("z")
    where = jnp.stack([my_x, my_c, my_y]).astype(jnp.int32)
    dim_model = section_inputs.shape[3]
    saved = section_inputs[0].reshape(-1, dim_model)
    down_map = adapter_down[0]
    up_map = adapter_up[0]
    heads = head_weights
    share, rank = heads.shape
    tok = representation.shape[1]
    column_task = jnp.repeat(head_task[:, 0], HEAD_OUT)
    mask = (column_task[None, :] == jnp.arange(rank, dtype=jnp.int32)[:, None]).astype(F32)

    piece = rows_at(heads, my_c * 128 + my_x * 32, 32)
    turn = [(a * NY + b, b * NY + a) for a in range(NX) for b in range(NY)]
    piece = lax.ppermute(piece, ("x", "y"), turn)

    blocks = representation[0].reshape(tok, NX, NZ, NC, 128).transpose(3, 1, 2, 0, 4)
    blocks = blocks.reshape(NC, NX, NZ * tok, 128)
    down_rows = rows_at(down_map, my_dp * share, share)
    swapped = swap_c(at(blocks, 1 - my_c))
    partner = swap_c(down_rows)
    pair = jnp.concatenate([at(blocks, my_c), swapped], axis=1)
    gots = []
    for k in range(1, NX):
        sent = jnp.concatenate([at(pair, (my_x - k) % NX), down_rows, partner], axis=0)
        gots.append(shift(sent, "x", -k))

    wide = dim_model // NY

    def cut(index, k, lo, size):
        return lax.dynamic_slice_in_dim(saved, ((index - k) % NY) * wide + lo, size, 1)

    x1 = shift(cut(my_y, 1, 0, wide), "y", -1)
    x3 = shift(cut(my_y, 3, 0, wide), "y", -3)

    up_rows = rows_at(up_map, my_dp * share, share)
    sent, factors, rep = local_call(
        pack_kernel,
        [((DP, 64, rank), BF16), ((SECTIONS, share, rank), BF16), ((SECTIONS, NZ * tok, rank), BF16)],
        where, piece, heads, up_rows, at(pair, my_x), down_rows, partner, *gots,
    )

    preact = jnp.dot(saved, down_map, preferred_element_type=F32)
    logistic = jax.nn.sigmoid(preact)
    active = (preact * logistic).astype(BF16)
    slope = (logistic * (1.0 + preact * (1.0 - logistic))).astype(BF16)
    slope_own = jnp.stack([slope] + [from_later(slope, k) for k in range(1, NX)])
    slope_other = swap_c(slope_own)

    late_y, sent = lax.optimization_barrier((my_y, sent))
    x2a = cut(late_y, 2, 0, wide // 2)
    x2b = cut(late_y, 2, wide // 2, wide // 2)
    got = exchange_dp(sent)
    part, cross_rows, _ = local_call(
        heads_kernel,
        [((384, rank), F32), ((32, rank), BF16), ((1024, rank), BF16)],
        where, got, rep, head_targets[0],
    )
    part = part + swap_c(part)
    top = part.astype(BF16)
    low = (part[256:] - top[256:].astype(F32)).astype(BF16)
    halves = jnp.concatenate([top, low], axis=0)
    others = [shift(halves, "x", -k) for k in range(1, NX)]
    x2a = shift(x2a, "y", -2)
    sent, residual = local_call(
        gram_kernel,
        [((DP, 48, rank), BF16), ((256, rank), BF16)],
        where, halves, *others, mask, cross_rows,
    )
    got = exchange_dp(sent)
    cross = got[:, :32].reshape(-1, rank)
    kept = [cross]
    for k in range(1, NX):
        kept.append(from_later(cross[: LATER_ROWS[k]], k))
    x2b = shift(x2b, "y", -2)
    cross_own = jnp.concatenate(kept, axis=0)
    cross_other = swap_c(cross_own)
    keep, send1, send2, send3, inner, mix, _ = local_call(
        chain_kernel,
        [((256, rank), BF16)] + [((512, rank), BF16)] * 3
        + [((256, rank), BF16), ((8, rank), F32), ((1024, rank), BF16)],
        where, got, mask, residual, active, cross_own, cross_other, slope_own, slope_other,
    )
    got1 = shift(send1, "y", -1)
    got2 = shift(send2, "y", -2)
    got3 = shift(send3, "y", -3)
    part_down = run_down(my_y, saved, x1, x2a, x2b, x3, inner, keep, got1, got2, got3)
    got = lax.all_to_all(part_down, "z", 0, 0, tiled=True)
    total = jnp.sum(got.astype(F32), axis=0)
    rows = total[256:].astype(BF16)
    middle = exchange_dp(jnp.broadcast_to(rows[None], (DP, 32, rank)))
    middle = middle.reshape(SECTIONS, rank, rank)
    grad_up = lax.dot_general(
        factors, middle, (((0, 2), (0, 2)), ((), ())), preferred_element_type=F32
    )
    grad_down = jnp.concatenate([total[:128].T, total[128:256].T], axis=0)
    return (grad_down[None], grad_up[None], mix[0, :TASKS])


def solution(mesh):
    fine = Mesh(mesh.devices.reshape(NX, NC, NY, NZ), ("x", "c", "y", "z"))
    section = ("x", "c")
    dp = ("y", "z")
    in_specs = (
        P(section, None, dp, None),
        P(section, None, None),
        P(section, None, None),
        P(section, dp, None),
        P(dp, None),
        P(section, dp, None),
        P(),
    )
    out_specs = (P(section, dp, None), P(section, dp, None), P())
    return jax.shard_map(stages, mesh=fine, in_specs=in_specs, out_specs=out_specs, check_vma=False)
```

```python
import jax
import jax.numpy as jnp
from jax import lax
from jax.experimental import pallas as pl
from jax.experimental.pallas import tpu as pltpu
from jax.sharding import Mesh
from jax.sharding import PartitionSpec as P


HEAD_OUT = 16
TASKS = 6
STEPS = 20
STEP_RATE = 3.0
NX = 4
NC = 2
NY = 4
NZ = 8
SECTIONS = NX * NC
DP = NY * NZ
BF16 = jnp.bfloat16
F32 = jnp.float32


def shift(value, axis, steps):
    count = lax.axis_size(axis)
    return lax.ppermute(value, axis, [(src, (src + steps) % count) for src in range(count)])


def from_later(value, steps):
    return lax.ppermute(value, "x", [(src, src - steps) for src in range(steps, NX)])


def swap_c(value):
    return lax.ppermute(value, "c", [(0, 1), (1, 0)])


def exchange_dp(blocks):
    return lax.all_to_all(blocks, ("y", "z"), 0, 0, tiled=True)


def at(value, index):
    return lax.dynamic_index_in_dim(value, index, 0, keepdims=False)


def rows_at(value, start, size):
    return lax.dynamic_slice_in_dim(value, start, size, 0)


def across(left, right):
    return lax.dot_general(left, right, (((0,), (0,)), ((), ())), preferred_element_type=F32)


VMEM = pl.BlockSpec(memory_space=pltpu.VMEM)
SMEM = pl.BlockSpec(memory_space=pltpu.SMEM)


def local_call(kernel, outs, where, *operands):
    return pl.pallas_call(
        kernel,
        out_shape=tuple(jax.ShapeDtypeStruct(shape, dtype) for shape, dtype in outs),
        in_specs=[SMEM] + [VMEM] * len(operands),
        out_specs=(VMEM,) * len(outs),
    )(where, *operands)


def pack_kernel(
    where_ref, piece_ref, heads_ref, up_ref, own_rep_ref, own_ref, partner_ref,
    got1_ref, got2_ref, got3_ref, sent_ref, factor_ref, rep_ref,
):
    my_x = where_ref[0]
    my_c = where_ref[1]
    my_stage = my_x * NC + my_c
    up_rows = up_ref[...]
    piece = piece_ref[...]
    for d in range(DP):
        sent_ref[d, 0:32, :] = piece
    gots = (None, got1_ref, got2_ref, got3_ref)
    for k in range(NX):
        for r in range(NC):
            stage = ((my_x + k) % NX) * NC + (my_c if r == 0 else 1 - my_c)
            slot = SECTIONS - 1 - stage
            if k == 0:
                rep_rows = own_rep_ref[256 * r : 256 * r + 256, :]
                factor = heads_ref[...] if r == 0 else partner_ref[...]
            else:
                rep_rows = gots[k][256 * r : 256 * r + 256, :]
                factor = gots[k][512 + 256 * r : 768 + 256 * r, :]
            if k or r:
                factor = jnp.where(stage > my_stage, factor, jnp.zeros_like(factor))
            rep_ref[stage] = rep_rows
            factor_ref[slot] = factor
            product = across(factor, up_rows).astype(BF16)
            for i in range(4):
                sent_ref[4 * slot + i, 32:64, :] = product[32 * i : 32 * i + 32]


def heads_kernel(where_ref, got_ref, rep_ref, target_ref, part_ref, cross_ref, head_ref):
    my_stage = where_ref[0] * NC + where_ref[1]
    for z in range(NZ):
        for y in range(NY):
            head_ref[128 * z + 32 * y : 128 * z + 32 * y + 32, :] = got_ref[NZ * y + z, 0:32, :]
    total = None
    square = None
    for z in range(NZ):
        head = head_ref[128 * z : 128 * z + 128, :]
        rep = jnp.concatenate([rep_ref[m, 32 * z : 32 * z + 32, :] for m in range(SECTIONS)], axis=0)
        term = jnp.dot(rep, head, preferred_element_type=F32)
        other = across(head, head)
        total = term if total is None else total + term
        square = other if square is None else square + other
    target = target_ref[...].astype(F32)
    for m in range(SECTIONS):
        rows = total[32 * m : 32 * m + 32]
        part_ref[32 * m : 32 * m + 32, :] = rows - jnp.where(m == my_stage, target, 0.0)
    part_ref[256:384, :] = square
    cross_ref[...] = jnp.sum(got_ref[:, 32:64, :].astype(F32), axis=0).astype(BF16)


def gram_kernel(where_ref, a_ref, b_ref, c_ref, d_ref, mask_ref, sent_ref, residual_ref):
    def value(ref, lo, size):
        return ref[lo : lo + size, :].astype(F32)

    def summed(lo, size):
        pair = value(a_ref, lo, size) + value(c_ref, lo, size)
        return pair + (value(b_ref, lo, size) + value(d_ref, lo, size))

    def squares(ref):
        return value(ref, 256, 128) + value(ref, 384, 128)

    residual = summed(0, 256).astype(BF16)
    residual_ref[...] = residual
    square = (squares(a_ref) + squares(c_ref)) + (squares(b_ref) + squares(d_ref))
    product = square * across(residual, residual)
    mask = mask_ref[...]
    high = lax.Precision.HIGHEST
    half = jnp.dot(mask[0:8], product, precision=high, preferred_element_type=F32)
    part = lax.dot_general(
        half, mask, (((1,), (1,)), ((), ())), precision=high, preferred_element_type=F32
    )
    top = part.astype(BF16)
    tile = jnp.concatenate([part, part - top.astype(F32)], axis=0).astype(BF16)
    for d in range(DP):
        sent_ref[d] = tile


LATER_ROWS = (1024, 768, 512, 256)
LATER_FROM = (0, 1024, 1792, 2304)
ALL_ROWS = 2560


def chain_kernel(
    where_ref, got_ref, mask_ref, residual_ref, active_ref, own_ref, other_ref,
    slope_own_ref, slope_other_ref,
    keep_ref, send1_ref, send2_ref, send3_ref, inner_ref, mix_ref, middle_ref,
):
    my_x = where_ref[0]
    my_c = where_ref[1]
    my_y = where_ref[2]
    my_stage = my_x * NC + my_c
    tiles = jnp.sum(got_ref[...].astype(F32), axis=0)
    gram = tiles[0:8] + tiles[8:16]
    rows = lax.broadcasted_iota(jnp.int32, gram.shape, 0)
    lanes = lax.broadcasted_iota(jnp.int32, gram.shape, 1)
    diagonal = jnp.where(rows == lanes, gram, 0.0)
    trace_sum = jnp.sum(jnp.sum(diagonal, axis=1, keepdims=True), axis=0, keepdims=True) + 1e-06
    scaled = gram * (-STEP_RATE / trace_sum)
    tasks = range(TASKS)
    entry = [[jnp.broadcast_to(scaled[t : t + 1, u : u + 1], (8, 128)) for u in tasks] for t in tasks]

    def advance(counter, weights):
        total = ((weights[0] + weights[1]) + (weights[2] + weights[3])) + (weights[4] + weights[5])
        inverse = 1.0 / total
        moved = []
        for t in tasks:
            terms = [entry[t][u] * weights[u] for u in tasks]
            step = ((terms[0] + terms[1]) + (terms[2] + terms[3])) + (terms[4] + terms[5])
            moved.append(weights[t] * jnp.exp(step * inverse))
        return tuple(moved)

    even = jnp.full((8, 128), 1.0 / TASKS, F32)
    weights = lax.fori_loop(0, STEPS, advance, (even,) * TASKS)
    total = ((weights[0] + weights[1]) + (weights[2] + weights[3])) + (weights[4] + weights[5])
    weights = [weight / total for weight in weights]
    mix = jnp.zeros((8, 128), F32)
    column_weight = jnp.zeros((1, 128), F32)
    for t in tasks:
        mix = jnp.where(lanes == t, weights[t], mix)
        column_weight = column_weight + weights[t][0:1] * mask_ref[t : t + 1]
    mix_ref[...] = mix

    def cross(stage, source):
        away = (stage // NC - my_x) % NX
        start = jnp.where(away == 0, LATER_FROM[0], LATER_FROM[1])
        start = jnp.where(away == 2, LATER_FROM[2], start)
        start = jnp.where(away == 3, LATER_FROM[3], start)
        start = jnp.minimum(start + 128 * (SECTIONS - 1 - source), ALL_ROWS - 128)
        start = pl.multiple_of(start, 128)
        own = own_ref[pl.ds(start, 128), :]
        return jnp.where(my_c == stage % NC, own, other_ref[pl.ds(start, 128), :])

    def slope_of(stage):
        away = (stage // NC - my_x) % NX
        return jnp.where(my_c == stage % NC, slope_own_ref[away], slope_other_ref[away])

    active = active_ref[...].T
    weighted = (residual_ref[...].astype(F32) * column_weight).astype(BF16)
    first = jnp.dot(active, weighted, preferred_element_type=F32)
    inners = {}
    for stage in range(SECTIONS - 1, -1, -1):
        left = [weighted] + [inners[s] for s in range(SECTIONS - 1, stage, -1)]
        right = [cross(stage, s) for s in [stage] + list(range(SECTIONS - 1, stage, -1))]
        branch = None
        for n in range(0, len(left), 2):
            term = jnp.dot(
                jnp.concatenate(left[n : n + 2], axis=1),
                jnp.concatenate(right[n : n + 2], axis=0),
                preferred_element_type=F32,
            )
            branch = term if branch is None else branch + term
        inner = (branch * slope_of(stage).astype(F32)).astype(BF16)
        inners[stage] = inner

        @pl.when(stage == my_stage)
        def _():
            inner_ref[...] = inner
            send1_ref[256:512, :] = inner
            send2_ref[256:512, :] = inner
            send3_ref[256:512, :] = inner

        product = jnp.dot(active, inner, preferred_element_type=F32)
        product = jnp.where(stage > my_stage, product, 0.0)
        product = jnp.where(stage == my_stage, first, product)
        lo = 128 * (SECTIONS - 1 - stage)
        middle_ref[lo : lo + 128, :] = product.astype(BF16)

    for k, ref in enumerate((keep_ref, send1_ref, send2_ref, send3_ref)):
        start = pl.multiple_of(((my_y - k) % NY) * 256, 256)
        ref[0:256, :] = middle_ref[pl.ds(start, 256), :]


def down_kernel(
    y_ref, x0_ref, x1_ref, x2a_ref, x2b_ref, x3_ref, inner_ref, keep_ref, got1_ref, got2_ref, got3_ref,
    out_ref,
):
    step = pl.program_id(0)
    x2 = jnp.where(step < 2, x2a_ref[...], x2b_ref[...])
    total = across(inner_ref[...], x0_ref[...])
    total = total + across(got1_ref[256:512, :], x1_ref[...])
    total = total + across(got2_ref[256:512, :], x2)
    total = total + across(got3_ref[256:512, :], x3_ref[...])
    total = total.astype(BF16)
    for j in range(2):
        for h in range(2):
            lo = 256 * j + 128 * h
            out_ref[j, 128 * h : 128 * h + 128, :] = total[:, lo : lo + 128]
        start = pl.multiple_of((2 * step + j) * 32, 32)
        rows = [ref[pl.ds(start, 32), :].astype(F32) for ref in (keep_ref, got1_ref, got2_ref, got3_ref)]
        out_ref[j, 256:288, :] = ((rows[0] + rows[1]) + (rows[2] + rows[3])).astype(BF16)


def run_down(my_y, saved, x1, x2a, x2b, x3, inner, keep, got1, got2, got3):
    cols = 512
    whole = lambda value: pl.BlockSpec(value.shape, lambda i, y: (0, 0))
    block = (256, cols)
    return pl.pallas_call(
        down_kernel,
        grid_spec=pltpu.PrefetchScalarGridSpec(
            num_scalar_prefetch=1,
            grid=(4,),
            in_specs=[
                pl.BlockSpec(block, lambda i, y: (0, 4 * y[0] + i)),
                pl.BlockSpec(block, lambda i, y: (0, i)),
                pl.BlockSpec(block, lambda i, y: (0, jnp.minimum(i, 1))),
                pl.BlockSpec(block, lambda i, y: (0, jnp.maximum(i - 2, 0))),
                pl.BlockSpec(block, lambda i, y: (0, i)),
                whole(inner), whole(keep), whole(got1), whole(got2), whole(got3),
            ],
            out_specs=pl.BlockSpec((2, 288, 128), lambda i, y: (i, 0, 0)),
        ),
        out_shape=jax.ShapeDtypeStruct((NZ, 288, 128), BF16),
        name="down_product",
    )(my_y.reshape(1), saved, x1, x2a, x2b, x3, inner, keep, got1, got2, got3)


def stages(
    section_inputs, adapter_down, adapter_up, representation, head_weights, head_targets, head_task
):
    my_x = lax.axis_index("x")
    my_c = lax.axis_index("c")
    my_y = lax.axis_index("y")
    my_dp = my_y * NZ + lax.axis_index("z")
    where = jnp.stack([my_x, my_c, my_y]).astype(jnp.int32)
    dim_model = section_inputs.shape[3]
    saved = section_inputs[0].reshape(-1, dim_model)
    down_map = adapter_down[0]
    up_map = adapter_up[0]
    heads = head_weights
    share, rank = heads.shape
    tok = representation.shape[1]
    column_task = jnp.repeat(head_task[:, 0], HEAD_OUT)
    mask = (column_task[None, :] == jnp.arange(rank, dtype=jnp.int32)[:, None]).astype(F32)

    piece = rows_at(heads, my_c * 128 + my_x * 32, 32)
    turn = [(a * NY + b, b * NY + a) for a in range(NX) for b in range(NY)]
    piece = lax.ppermute(piece, ("x", "y"), turn)

    blocks = representation[0].reshape(tok, NX, NZ, NC, 128).transpose(3, 1, 2, 0, 4)
    blocks = blocks.reshape(NC, NX, NZ * tok, 128)
    down_rows = rows_at(down_map, my_dp * share, share)
    swapped = swap_c(at(blocks, 1 - my_c))
    partner = swap_c(down_rows)
    pair = jnp.concatenate([at(blocks, my_c), swapped], axis=1)
    gots = []
    for k in range(1, NX):
        sent = jnp.concatenate([at(pair, (my_x - k) % NX), down_rows, partner], axis=0)
        gots.append(shift(sent, "x", -k))

    wide = dim_model // NY

    def cut(index, k, lo, size):
        return lax.dynamic_slice_in_dim(saved, ((index - k) % NY) * wide + lo, size, 1)

    x1 = shift(cut(my_y, 1, 0, wide), "y", -1)
    x3 = shift(cut(my_y, 3, 0, wide), "y", -3)

    up_rows = rows_at(up_map, my_dp * share, share)
    sent, factors, rep = local_call(
        pack_kernel,
        [((DP, 64, rank), BF16), ((SECTIONS, share, rank), BF16), ((SECTIONS, NZ * tok, rank), BF16)],
        where, piece, heads, up_rows, at(pair, my_x), down_rows, partner, *gots,
    )

    late_y, down_late, sent = lax.optimization_barrier((my_y, down_map, sent))
    x2a = cut(late_y, 2, 0, wide // 2)
    x2b = cut(late_y, 2, wide // 2, wide // 2)
    preact = jnp.dot(saved, down_late, preferred_element_type=F32)
    logistic = jax.nn.sigmoid(preact)
    active = (preact * logistic).astype(BF16)
    slope = (logistic * (1.0 + preact * (1.0 - logistic))).astype(BF16)
    slope_own = jnp.stack([slope] + [from_later(slope, k) for k in range(1, NX)])
    slope_other = swap_c(slope_own)

    got = exchange_dp(sent)
    part, cross_rows, _ = local_call(
        heads_kernel,
        [((384, rank), F32), ((32, rank), BF16), ((1024, rank), BF16)],
        where, got, rep, head_targets[0],
    )
    got = exchange_dp(jnp.broadcast_to(cross_rows[None], (DP, 32, rank)))
    cross = got.reshape(-1, rank)
    kept = [cross]
    for k in range(1, NX):
        kept.append(from_later(cross[: LATER_ROWS[k]], k))
    part = part + swap_c(part)
    top = part.astype(BF16)
    low = (part[256:] - top[256:].astype(F32)).astype(BF16)
    halves = jnp.concatenate([top, low], axis=0)
    others = [shift(halves, "x", -k) for k in range(1, NX)]
    x2a = shift(x2a, "y", -2)
    sent, residual = local_call(
        gram_kernel,
        [((DP, 16, rank), BF16), ((256, rank), BF16)],
        where, halves, *others, mask,
    )
    got = exchange_dp(sent)
    x2b = shift(x2b, "y", -2)
    cross_own = jnp.concatenate(kept, axis=0)
    cross_other = swap_c(cross_own)
    keep, send1, send2, send3, inner, mix, _ = local_call(
        chain_kernel,
        [((256, rank), BF16)] + [((512, rank), BF16)] * 3
        + [((256, rank), BF16), ((8, rank), F32), ((1024, rank), BF16)],
        where, got, mask, residual, active, cross_own, cross_other, slope_own, slope_other,
    )
    got1 = shift(send1, "y", -1)
    got2 = shift(send2, "y", -2)
    got3 = shift(send3, "y", -3)
    part_down = run_down(my_y, saved, x1, x2a, x2b, x3, inner, keep, got1, got2, got3)
    got = lax.all_to_all(part_down, "z", 0, 0, tiled=True)
    total = jnp.sum(got.astype(F32), axis=0)
    rows = total[256:].astype(BF16)
    middle = exchange_dp(jnp.broadcast_to(rows[None], (DP, 32, rank)))
    middle = middle.reshape(SECTIONS, rank, rank)
    grad_up = lax.dot_general(
        factors, middle, (((0, 2), (0, 2)), ((), ())), preferred_element_type=F32
    )
    grad_down = jnp.concatenate([total[:128].T, total[128:256].T], axis=0)
    return (grad_down[None], grad_up[None], mix[0, :TASKS])


def solution(mesh):
    fine = Mesh(mesh.devices.reshape(NX, NC, NY, NZ), ("x", "c", "y", "z"))
    section = ("x", "c")
    dp = ("y", "z")
    in_specs = (
        P(section, None, dp, None),
        P(section, None, None),
        P(section, None, None),
        P(section, dp, None),
        P(dp, None),
        P(section, dp, None),
        P(),
    )
    out_specs = (P(section, dp, None), P(section, dp, None), P())
    return jax.shard_map(stages, mesh=fine, in_specs=in_specs, out_specs=out_specs, check_vma=False)
```

```python
import jax
import jax.numpy as jnp
from jax import lax
from jax.experimental import pallas as pl
from jax.experimental.pallas import tpu as pltpu
from jax.sharding import Mesh
from jax.sharding import PartitionSpec as P


HEAD_OUT = 16
TASKS = 6
STEPS = 20
STEP_RATE = 3.0
NX = 4
NC = 2
NY = 4
NZ = 8
SECTIONS = NX * NC
DP = NY * NZ
BF16 = jnp.bfloat16
F32 = jnp.float32


def shift(value, axis, steps):
    count = lax.axis_size(axis)
    return lax.ppermute(value, axis, [(src, (src + steps) % count) for src in range(count)])


def from_later(value, steps):
    return lax.ppermute(value, "x", [(src, src - steps) for src in range(steps, NX)])


def swap_c(value):
    return lax.ppermute(value, "c", [(0, 1), (1, 0)])


def exchange_dp(blocks):
    return lax.all_to_all(blocks, ("y", "z"), 0, 0, tiled=True)


def at(value, index):
    return lax.dynamic_index_in_dim(value, index, 0, keepdims=False)


def rows_at(value, start, size):
    return lax.dynamic_slice_in_dim(value, start, size, 0)


def across(left, right):
    return lax.dot_general(left, right, (((0,), (0,)), ((), ())), preferred_element_type=F32)


VMEM = pl.BlockSpec(memory_space=pltpu.VMEM)
SMEM = pl.BlockSpec(memory_space=pltpu.SMEM)


def local_call(kernel, outs, where, *operands):
    return pl.pallas_call(
        kernel,
        out_shape=tuple(jax.ShapeDtypeStruct(shape, dtype) for shape, dtype in outs),
        in_specs=[SMEM] + [VMEM] * len(operands),
        out_specs=(VMEM,) * len(outs),
    )(where, *operands)


def pack_kernel(
    where_ref, piece_ref, heads_ref, up_ref, own_rep_ref, own_ref, partner_ref,
    got1_ref, got2_ref, got3_ref, sent_ref, factor_ref, rep_ref,
):
    my_x = where_ref[0]
    my_c = where_ref[1]
    my_stage = my_x * NC + my_c
    up_rows = up_ref[...]
    piece = piece_ref[...]
    for d in range(DP):
        sent_ref[d, 0:32, :] = piece
    gots = (None, got1_ref, got2_ref, got3_ref)
    for k in range(NX):
        for r in range(NC):
            stage = ((my_x + k) % NX) * NC + (my_c if r == 0 else 1 - my_c)
            slot = SECTIONS - 1 - stage
            if k == 0:
                rep_rows = own_rep_ref[256 * r : 256 * r + 256, :]
                factor = heads_ref[...] if r == 0 else partner_ref[...]
            else:
                rep_rows = gots[k][256 * r : 256 * r + 256, :]
                factor = gots[k][512 + 256 * r : 768 + 256 * r, :]
            if k or r:
                factor = jnp.where(stage > my_stage, factor, jnp.zeros_like(factor))
            rep_ref[stage] = rep_rows
            factor_ref[slot] = factor
            product = across(factor, up_rows).astype(BF16)
            for i in range(4):
                sent_ref[4 * slot + i, 32:64, :] = product[32 * i : 32 * i + 32]


def heads_kernel(where_ref, got_ref, rep_ref, target_ref, part_ref, cross_ref, head_ref):
    my_stage = where_ref[0] * NC + where_ref[1]
    for z in range(NZ):
        for y in range(NY):
            head_ref[128 * z + 32 * y : 128 * z + 32 * y + 32, :] = got_ref[NZ * y + z, 0:32, :]
    total = None
    square = None
    for z in range(NZ):
        head = head_ref[128 * z : 128 * z + 128, :]
        rep = jnp.concatenate([rep_ref[m, 32 * z : 32 * z + 32, :] for m in range(SECTIONS)], axis=0)
        term = jnp.dot(rep, head, preferred_element_type=F32)
        other = across(head, head)
        total = term if total is None else total + term
        square = other if square is None else square + other
    target = target_ref[...].astype(F32)
    for m in range(SECTIONS):
        rows = total[32 * m : 32 * m + 32]
        part_ref[32 * m : 32 * m + 32, :] = rows - jnp.where(m == my_stage, target, 0.0)
    part_ref[256:384, :] = square
    cross = jnp.sum(got_ref[:, 32:64, :].astype(F32), axis=0).astype(BF16)
    for d in range(DP):
        cross_ref[d] = cross


def gram_kernel(where_ref, a_ref, b_ref, c_ref, d_ref, mask_ref, sent_ref, residual_ref):
    def value(ref, lo, size):
        return ref[lo : lo + size, :].astype(F32)

    def summed(lo, size):
        pair = value(a_ref, lo, size) + value(c_ref, lo, size)
        return pair + (value(b_ref, lo, size) + value(d_ref, lo, size))

    def squares(ref):
        return value(ref, 256, 128) + value(ref, 384, 128)

    residual = summed(0, 256).astype(BF16)
    residual_ref[...] = residual
    square = (squares(a_ref) + squares(c_ref)) + (squares(b_ref) + squares(d_ref))
    product = square * across(residual, residual)
    mask = mask_ref[...]
    high = lax.Precision.HIGHEST
    half = jnp.dot(mask[0:8], product, precision=high, preferred_element_type=F32)
    part = lax.dot_general(
        half, mask, (((1,), (1,)), ((), ())), precision=high, preferred_element_type=F32
    )
    top = part.astype(BF16)
    tile = jnp.concatenate([part, part - top.astype(F32)], axis=0).astype(BF16)
    for d in range(DP):
        sent_ref[d] = tile


LATER_ROWS = (1024, 768, 512, 256)
LATER_FROM = (0, 1024, 1792, 2304)
ALL_ROWS = 2560


def chain_kernel(
    where_ref, got_ref, mask_ref, residual_ref, active_ref, own_ref, other_ref,
    slope_own_ref, slope_other_ref,
    keep_ref, send1_ref, send2_ref, send3_ref, inner_ref, mix_ref, middle_ref,
):
    my_x = where_ref[0]
    my_c = where_ref[1]
    my_y = where_ref[2]
    my_stage = my_x * NC + my_c
    tiles = jnp.sum(got_ref[...].astype(F32), axis=0)
    gram = tiles[0:8] + tiles[8:16]
    rows = lax.broadcasted_iota(jnp.int32, gram.shape, 0)
    lanes = lax.broadcasted_iota(jnp.int32, gram.shape, 1)
    diagonal = jnp.where(rows == lanes, gram, 0.0)
    trace_sum = jnp.sum(jnp.sum(diagonal, axis=1, keepdims=True), axis=0, keepdims=True) + 1e-06
    scaled = gram * (-STEP_RATE / trace_sum)
    tasks = range(TASKS)
    entry = [[jnp.broadcast_to(scaled[t : t + 1, u : u + 1], (8, 128)) for u in tasks] for t in tasks]

    def advance(counter, weights):
        total = ((weights[0] + weights[1]) + (weights[2] + weights[3])) + (weights[4] + weights[5])
        inverse = 1.0 / total
        moved = []
        for t in tasks:
            terms = [entry[t][u] * weights[u] for u in tasks]
            step = ((terms[0] + terms[1]) + (terms[2] + terms[3])) + (terms[4] + terms[5])
            moved.append(weights[t] * jnp.exp(step * inverse))
        return tuple(moved)

    even = jnp.full((8, 128), 1.0 / TASKS, F32)
    weights = lax.fori_loop(0, STEPS, advance, (even,) * TASKS)
    total = ((weights[0] + weights[1]) + (weights[2] + weights[3])) + (weights[4] + weights[5])
    weights = [weight / total for weight in weights]
    mix = jnp.zeros((8, 128), F32)
    column_weight = jnp.zeros((1, 128), F32)
    for t in tasks:
        mix = jnp.where(lanes == t, weights[t], mix)
        column_weight = column_weight + weights[t][0:1] * mask_ref[t : t + 1]
    mix_ref[...] = mix

    def cross(stage, source):
        away = (stage // NC - my_x) % NX
        start = jnp.where(away == 0, LATER_FROM[0], LATER_FROM[1])
        start = jnp.where(away == 2, LATER_FROM[2], start)
        start = jnp.where(away == 3, LATER_FROM[3], start)
        start = jnp.minimum(start + 128 * (SECTIONS - 1 - source), ALL_ROWS - 128)
        start = pl.multiple_of(start, 128)
        own = own_ref[pl.ds(start, 128), :]
        return jnp.where(my_c == stage % NC, own, other_ref[pl.ds(start, 128), :])

    def slope_of(stage):
        away = (stage // NC - my_x) % NX
        return jnp.where(my_c == stage % NC, slope_own_ref[away], slope_other_ref[away])

    active = active_ref[...].T
    weighted = (residual_ref[...].astype(F32) * column_weight).astype(BF16)
    first = jnp.dot(active, weighted, preferred_element_type=F32)
    inners = {}
    for stage in range(SECTIONS - 1, -1, -1):
        left = [weighted] + [inners[s] for s in range(SECTIONS - 1, stage, -1)]
        right = [cross(stage, s) for s in [stage] + list(range(SECTIONS - 1, stage, -1))]
        branch = None
        for n in range(0, len(left), 2):
            term = jnp.dot(
                jnp.concatenate(left[n : n + 2], axis=1),
                jnp.concatenate(right[n : n + 2], axis=0),
                preferred_element_type=F32,
            )
            branch = term if branch is None else branch + term
        inner = (branch * slope_of(stage).astype(F32)).astype(BF16)
        inners[stage] = inner

        @pl.when(stage == my_stage)
        def _():
            inner_ref[...] = inner
            send1_ref[256:512, :] = inner
            send2_ref[256:512, :] = inner
            send3_ref[256:512, :] = inner

        product = jnp.dot(active, inner, preferred_element_type=F32)
        product = jnp.where(stage > my_stage, product, 0.0)
        product = jnp.where(stage == my_stage, first, product)
        lo = 128 * (SECTIONS - 1 - stage)
        middle_ref[lo : lo + 128, :] = product.astype(BF16)

    for k, ref in enumerate((keep_ref, send1_ref, send2_ref, send3_ref)):
        start = pl.multiple_of(((my_y - k) % NY) * 256, 256)
        ref[0:256, :] = middle_ref[pl.ds(start, 256), :]


def down_kernel(
    y_ref, x0_ref, x1_ref, x2a_ref, x2b_ref, x3_ref, inner_ref, keep_ref, got1_ref, got2_ref, got3_ref,
    out_ref,
):
    step = pl.program_id(0)
    x2 = jnp.where(step < 2, x2a_ref[...], x2b_ref[...])
    total = across(inner_ref[...], x0_ref[...])
    total = total + across(got1_ref[256:512, :], x1_ref[...])
    total = total + across(got2_ref[256:512, :], x2)
    total = total + across(got3_ref[256:512, :], x3_ref[...])
    total = total.astype(BF16)
    for j in range(2):
        for h in range(2):
            lo = 256 * j + 128 * h
            out_ref[j, 128 * h : 128 * h + 128, :] = total[:, lo : lo + 128]
        start = pl.multiple_of((2 * step + j) * 32, 32)
        rows = [ref[pl.ds(start, 32), :].astype(F32) for ref in (keep_ref, got1_ref, got2_ref, got3_ref)]
        out_ref[j, 256:288, :] = ((rows[0] + rows[1]) + (rows[2] + rows[3])).astype(BF16)


def run_down(my_y, saved, x1, x2a, x2b, x3, inner, keep, got1, got2, got3):
    cols = 512
    whole = lambda value: pl.BlockSpec(value.shape, lambda i, y: (0, 0))
    block = (256, cols)
    return pl.pallas_call(
        down_kernel,
        grid_spec=pltpu.PrefetchScalarGridSpec(
            num_scalar_prefetch=1,
            grid=(4,),
            in_specs=[
                pl.BlockSpec(block, lambda i, y: (0, 4 * y[0] + i)),
                pl.BlockSpec(block, lambda i, y: (0, i)),
                pl.BlockSpec(block, lambda i, y: (0, jnp.minimum(i, 1))),
                pl.BlockSpec(block, lambda i, y: (0, jnp.maximum(i - 2, 0))),
                pl.BlockSpec(block, lambda i, y: (0, i)),
                whole(inner), whole(keep), whole(got1), whole(got2), whole(got3),
            ],
            out_specs=pl.BlockSpec((2, 288, 128), lambda i, y: (i, 0, 0)),
        ),
        out_shape=jax.ShapeDtypeStruct((NZ, 288, 128), BF16),
        name="down_product",
    )(my_y.reshape(1), saved, x1, x2a, x2b, x3, inner, keep, got1, got2, got3)


def stages(
    section_inputs, adapter_down, adapter_up, representation, head_weights, head_targets, head_task
):
    my_x = lax.axis_index("x")
    my_c = lax.axis_index("c")
    my_y = lax.axis_index("y")
    my_dp = my_y * NZ + lax.axis_index("z")
    where = jnp.stack([my_x, my_c, my_y]).astype(jnp.int32)
    dim_model = section_inputs.shape[3]
    saved = section_inputs[0].reshape(-1, dim_model)
    down_map = adapter_down[0]
    up_map = adapter_up[0]
    heads = head_weights
    share, rank = heads.shape
    tok = representation.shape[1]
    column_task = jnp.repeat(head_task[:, 0], HEAD_OUT)
    mask = (column_task[None, :] == jnp.arange(rank, dtype=jnp.int32)[:, None]).astype(F32)

    piece = rows_at(heads, my_c * 128 + my_x * 32, 32)
    turn = [(a * NY + b, b * NY + a) for a in range(NX) for b in range(NY)]
    piece = lax.ppermute(piece, ("x", "y"), turn)

    columns = representation[0].reshape(tok, NX * NZ, NC, 128)

    def half_of(core):
        taken = lax.dynamic_index_in_dim(columns, core, 2, keepdims=False)
        return taken.transpose(1, 0, 2).reshape(NX, NZ * tok, 128)

    down_rows = rows_at(down_map, my_dp * share, share)
    swapped = swap_c(half_of(1 - my_c))
    partner = swap_c(down_rows)
    pair = jnp.concatenate([half_of(my_c), swapped], axis=1)
    gots = []
    for k in range(1, NX):
        sent = jnp.concatenate([at(pair, (my_x - k) % NX), down_rows, partner], axis=0)
        gots.append(shift(sent, "x", -k))

    wide = dim_model // NY

    def cut(index, k, lo, size):
        return lax.dynamic_slice_in_dim(saved, ((index - k) % NY) * wide + lo, size, 1)

    x1 = cut(my_y, 1, 0, wide)
    x3 = cut(my_y, 3, 0, wide)
    x1 = shift(x1, "y", -1)
    x3 = shift(x3, "y", -3)

    up_rows = rows_at(up_map, my_dp * share, share)
    sent, factors, rep = local_call(
        pack_kernel,
        [((DP, 64, rank), BF16), ((SECTIONS, share, rank), BF16), ((SECTIONS, NZ * tok, rank), BF16)],
        where, piece, heads, up_rows, at(pair, my_x), down_rows, partner, *gots,
    )

    late_y, down_late, sent = lax.optimization_barrier((my_y, down_map, sent))
    x2a = cut(late_y, 2, 0, wide // 2)
    x2b = cut(late_y, 2, wide // 2, wide // 2)
    preact = jnp.dot(saved, down_late, preferred_element_type=F32)
    logistic = jax.nn.sigmoid(preact)
    active = (preact * logistic).astype(BF16)
    slope = (logistic * (1.0 + preact * (1.0 - logistic))).astype(BF16)
    slope_own = jnp.stack([slope] + [from_later(slope, k) for k in range(1, NX)])
    slope_other = swap_c(slope_own)

    got = exchange_dp(sent)
    part, cross_rows, _ = local_call(
        heads_kernel,
        [((384, rank), F32), ((DP, 32, rank), BF16), ((1024, rank), BF16)],
        where, got, rep, head_targets[0],
    )
    got = exchange_dp(cross_rows)
    cross = got.reshape(-1, rank)
    kept = [cross]
    for k in range(1, NX):
        kept.append(from_later(cross[: LATER_ROWS[k]], k))
    part = part + swap_c(part)
    top = part.astype(BF16)
    low = (part[256:] - top[256:].astype(F32)).astype(BF16)
    halves = jnp.concatenate([top, low], axis=0)
    others = [shift(halves, "x", -k) for k in range(1, NX)]
    x2a = shift(x2a, "y", -2)
    sent, residual = local_call(
        gram_kernel,
        [((DP, 16, rank), BF16), ((256, rank), BF16)],
        where, halves, *others, mask,
    )
    got = exchange_dp(sent)
    x2b = shift(x2b, "y", -2)
    cross_own = jnp.concatenate(kept, axis=0)
    cross_other = swap_c(cross_own)
    keep, send1, send2, send3, inner, mix, _ = local_call(
        chain_kernel,
        [((256, rank), BF16)] + [((512, rank), BF16)] * 3
        + [((256, rank), BF16), ((8, rank), F32), ((1024, rank), BF16)],
        where, got, mask, residual, active, cross_own, cross_other, slope_own, slope_other,
    )
    got1 = shift(send1, "y", -1)
    got2 = shift(send2, "y", -2)
    got3 = shift(send3, "y", -3)
    part_down = run_down(my_y, saved, x1, x2a, x2b, x3, inner, keep, got1, got2, got3)
    got = lax.all_to_all(part_down, "z", 0, 0, tiled=True)
    total = jnp.sum(got.astype(F32), axis=0)
    rows = total[256:].astype(BF16)
    middle = exchange_dp(jnp.broadcast_to(rows[None], (DP, 32, rank)))
    middle = middle.reshape(SECTIONS, rank, rank)
    grad_up = lax.dot_general(
        factors, middle, (((0, 2), (0, 2)), ((), ())), preferred_element_type=F32
    )
    grad_down = jnp.concatenate([total[:128].T, total[128:256].T], axis=0)
    return (grad_down[None], grad_up[None], mix[0, :TASKS])


def solution(mesh):
    fine = Mesh(mesh.devices.reshape(NX, NC, NY, NZ), ("x", "c", "y", "z"))
    section = ("x", "c")
    dp = ("y", "z")
    in_specs = (
        P(section, None, dp, None),
        P(section, None, None),
        P(section, None, None),
        P(section, dp, None),
        P(dp, None),
        P(section, dp, None),
        P(),
    )
    out_specs = (P(section, dp, None), P(section, dp, None), P())
    return jax.shard_map(stages, mesh=fine, in_specs=in_specs, out_specs=out_specs, check_vma=False)
```

```python
import jax
import jax.numpy as jnp
from jax import lax
from jax.experimental import pallas as pl
from jax.experimental.pallas import tpu as pltpu
from jax.sharding import Mesh
from jax.sharding import PartitionSpec as P


HEAD_OUT = 16
TASKS = 6
STEPS = 20
STEP_RATE = 3.0
NX = 4
NC = 2
NY = 4
NZ = 8
SECTIONS = NX * NC
DP = NY * NZ
BF16 = jnp.bfloat16
F32 = jnp.float32


def shift(value, axis, steps):
    count = lax.axis_size(axis)
    return lax.ppermute(value, axis, [(src, (src + steps) % count) for src in range(count)])


def from_later(value, steps):
    return lax.ppermute(value, "x", [(src, src - steps) for src in range(steps, NX)])


def swap_c(value):
    return lax.ppermute(value, "c", [(0, 1), (1, 0)])


def exchange_dp(blocks):
    return lax.all_to_all(blocks, ("y", "z"), 0, 0, tiled=True)


def at(value, index):
    return lax.dynamic_index_in_dim(value, index, 0, keepdims=False)


def rows_at(value, start, size):
    return lax.dynamic_slice_in_dim(value, start, size, 0)


def across(left, right):
    return lax.dot_general(left, right, (((0,), (0,)), ((), ())), preferred_element_type=F32)


VMEM = pl.BlockSpec(memory_space=pltpu.VMEM)
SMEM = pl.BlockSpec(memory_space=pltpu.SMEM)


def local_call(kernel, outs, where, *operands):
    return pl.pallas_call(
        kernel,
        out_shape=tuple(jax.ShapeDtypeStruct(shape, dtype) for shape, dtype in outs),
        in_specs=[SMEM] + [VMEM] * len(operands),
        out_specs=(VMEM,) * len(outs),
    )(where, *operands)


def pack_kernel(
    where_ref, piece_ref, heads_ref, up_ref, own_rep_ref, own_ref, partner_ref,
    got1_ref, got2_ref, got3_ref, sent_ref, factor_ref, rep_ref,
):
    my_x = where_ref[0]
    my_c = where_ref[1]
    my_stage = my_x * NC + my_c
    up_rows = up_ref[...]
    piece = piece_ref[...]
    for d in range(DP):
        sent_ref[d, 0:32, :] = piece
    gots = (None, got1_ref, got2_ref, got3_ref)
    for k in range(NX):
        for r in range(NC):
            stage = ((my_x + k) % NX) * NC + (my_c if r == 0 else 1 - my_c)
            slot = SECTIONS - 1 - stage
            if k == 0:
                rep_rows = own_rep_ref[256 * r : 256 * r + 256, :]
                factor = heads_ref[...] if r == 0 else partner_ref[...]
            else:
                rep_rows = gots[k][256 * r : 256 * r + 256, :]
                factor = gots[k][512 + 256 * r : 768 + 256 * r, :]
            if k or r:
                factor = jnp.where(stage > my_stage, factor, jnp.zeros_like(factor))
            rep_ref[stage] = rep_rows
            factor_ref[slot] = factor
            product = across(factor, up_rows).astype(BF16)
            for i in range(4):
                sent_ref[4 * slot + i, 32:64, :] = product[32 * i : 32 * i + 32]


def heads_kernel(where_ref, got_ref, rep_ref, target_ref, part_ref, cross_ref, head_ref):
    my_stage = where_ref[0] * NC + where_ref[1]
    for z in range(NZ):
        for y in range(NY):
            head_ref[128 * z + 32 * y : 128 * z + 32 * y + 32, :] = got_ref[NZ * y + z, 0:32, :]
    total = None
    square = None
    for z in range(NZ):
        head = head_ref[128 * z : 128 * z + 128, :]
        rep = jnp.concatenate([rep_ref[m, 32 * z : 32 * z + 32, :] for m in range(SECTIONS)], axis=0)
        term = jnp.dot(rep, head, preferred_element_type=F32)
        other = across(head, head)
        total = term if total is None else total + term
        square = other if square is None else square + other
    target = target_ref[...].astype(F32)
    for m in range(SECTIONS):
        rows = total[32 * m : 32 * m + 32]
        part_ref[32 * m : 32 * m + 32, :] = rows - jnp.where(m == my_stage, target, 0.0)
    part_ref[256:384, :] = square
    cross_ref[...] = jnp.sum(got_ref[:, 32:64, :].astype(F32), axis=0).astype(BF16)


def gram_kernel(where_ref, a_ref, b_ref, c_ref, d_ref, mask_ref, sent_ref, residual_ref):
    def value(ref, lo, size):
        return ref[lo : lo + size, :].astype(F32)

    def summed(lo, size):
        pair = value(a_ref, lo, size) + value(c_ref, lo, size)
        return pair + (value(b_ref, lo, size) + value(d_ref, lo, size))

    def squares(ref):
        return value(ref, 256, 128) + value(ref, 384, 128)

    residual = summed(0, 256).astype(BF16)
    residual_ref[...] = residual
    square = (squares(a_ref) + squares(c_ref)) + (squares(b_ref) + squares(d_ref))
    product = square * across(residual, residual)
    mask = mask_ref[...]
    high = lax.Precision.HIGHEST
    half = jnp.dot(mask[0:8], product, precision=high, preferred_element_type=F32)
    part = lax.dot_general(
        half, mask, (((1,), (1,)), ((), ())), precision=high, preferred_element_type=F32
    )
    top = part.astype(BF16)
    tile = jnp.concatenate([part, part - top.astype(F32)], axis=0).astype(BF16)
    for d in range(DP):
        sent_ref[d] = tile


LATER_ROWS = (1024, 768, 512, 256)
LATER_FROM = (0, 1024, 1792, 2304)
ALL_ROWS = 2560


def chain_kernel(
    where_ref, got_ref, mask_ref, residual_ref, active_ref, own_ref, other_ref,
    slope_own_ref, slope_other_ref,
    keep_ref, send1_ref, send2_ref, send3_ref, inner_ref, mix_ref, middle_ref,
):
    my_x = where_ref[0]
    my_c = where_ref[1]
    my_y = where_ref[2]
    my_stage = my_x * NC + my_c
    tiles = jnp.sum(got_ref[...].astype(F32), axis=0)
    gram = tiles[0:8] + tiles[8:16]
    rows = lax.broadcasted_iota(jnp.int32, gram.shape, 0)
    lanes = lax.broadcasted_iota(jnp.int32, gram.shape, 1)
    diagonal = jnp.where(rows == lanes, gram, 0.0)
    trace_sum = jnp.sum(jnp.sum(diagonal, axis=1, keepdims=True), axis=0, keepdims=True) + 1e-06
    scaled = gram * (-STEP_RATE / trace_sum)
    tasks = range(TASKS)
    entry = [[jnp.broadcast_to(scaled[t : t + 1, u : u + 1], (8, 128)) for u in tasks] for t in tasks]

    def advance(counter, weights):
        total = ((weights[0] + weights[1]) + (weights[2] + weights[3])) + (weights[4] + weights[5])
        inverse = 1.0 / total
        moved = []
        for t in tasks:
            terms = [entry[t][u] * weights[u] for u in tasks]
            step = ((terms[0] + terms[1]) + (terms[2] + terms[3])) + (terms[4] + terms[5])
            moved.append(weights[t] * jnp.exp(step * inverse))
        return tuple(moved)

    even = jnp.full((8, 128), 1.0 / TASKS, F32)
    weights = lax.fori_loop(0, STEPS, advance, (even,) * TASKS)
    total = ((weights[0] + weights[1]) + (weights[2] + weights[3])) + (weights[4] + weights[5])
    weights = [weight / total for weight in weights]
    mix = jnp.zeros((8, 128), F32)
    column_weight = jnp.zeros((1, 128), F32)
    for t in tasks:
        mix = jnp.where(lanes == t, weights[t], mix)
        column_weight = column_weight + weights[t][0:1] * mask_ref[t : t + 1]
    mix_ref[...] = mix

    def cross(stage, source):
        away = (stage // NC - my_x) % NX
        start = jnp.where(away == 0, LATER_FROM[0], LATER_FROM[1])
        start = jnp.where(away == 2, LATER_FROM[2], start)
        start = jnp.where(away == 3, LATER_FROM[3], start)
        start = jnp.minimum(start + 128 * (SECTIONS - 1 - source), ALL_ROWS - 128)
        start = pl.multiple_of(start, 128)
        own = own_ref[pl.ds(start, 128), :]
        return jnp.where(my_c == stage % NC, own, other_ref[pl.ds(start, 128), :])

    def slope_of(stage):
        away = (stage // NC - my_x) % NX
        return jnp.where(my_c == stage % NC, slope_own_ref[away], slope_other_ref[away])

    active = active_ref[...].T
    weighted = (residual_ref[...].astype(F32) * column_weight).astype(BF16)
    first = jnp.dot(active, weighted, preferred_element_type=F32)
    inners = {}
    for stage in range(SECTIONS - 1, -1, -1):
        left = [weighted] + [inners[s] for s in range(SECTIONS - 1, stage, -1)]
        right = [cross(stage, s) for s in [stage] + list(range(SECTIONS - 1, stage, -1))]
        branch = None
        for n in range(0, len(left), 2):
            term = jnp.dot(
                jnp.concatenate(left[n : n + 2], axis=1),
                jnp.concatenate(right[n : n + 2], axis=0),
                preferred_element_type=F32,
            )
            branch = term if branch is None else branch + term
        inner = (branch * slope_of(stage).astype(F32)).astype(BF16)
        inners[stage] = inner

        @pl.when(stage == my_stage)
        def _():
            inner_ref[...] = inner
            send1_ref[256:512, :] = inner
            send2_ref[256:512, :] = inner
            send3_ref[256:512, :] = inner

        product = jnp.dot(active, inner, preferred_element_type=F32)
        product = jnp.where(stage > my_stage, product, 0.0)
        product = jnp.where(stage == my_stage, first, product)
        lo = 128 * (SECTIONS - 1 - stage)
        middle_ref[lo : lo + 128, :] = product.astype(BF16)

    for k, ref in enumerate((keep_ref, send1_ref, send2_ref, send3_ref)):
        start = pl.multiple_of(((my_y - k) % NY) * 256, 256)
        ref[0:256, :] = middle_ref[pl.ds(start, 256), :]


def down_kernel(
    y_ref, x0_ref, x1_ref, x2_ref, x3_ref, inner_ref, keep_ref, got1_ref, got2_ref, got3_ref,
    out_ref,
):
    step = pl.program_id(0)
    total = across(inner_ref[...], x0_ref[...])
    total = total + across(got1_ref[256:512, :], x1_ref[...])
    total = total + across(got2_ref[256:512, :], x2_ref[...])
    total = total + across(got3_ref[256:512, :], x3_ref[...])
    total = total.astype(BF16)
    for j in range(2):
        for h in range(2):
            lo = 256 * j + 128 * h
            out_ref[j, 128 * h : 128 * h + 128, :] = total[:, lo : lo + 128]
        start = pl.multiple_of((2 * step + j) * 32, 32)
        rows = [ref[pl.ds(start, 32), :].astype(F32) for ref in (keep_ref, got1_ref, got2_ref, got3_ref)]
        out_ref[j, 256:288, :] = ((rows[0] + rows[1]) + (rows[2] + rows[3])).astype(BF16)


def run_down(my_y, saved, x1, x2, x3, inner, keep, got1, got2, got3):
    cols = 512
    whole = lambda value: pl.BlockSpec(value.shape, lambda i, y: (0, 0))
    block = (256, cols)
    return pl.pallas_call(
        down_kernel,
        grid_spec=pltpu.PrefetchScalarGridSpec(
            num_scalar_prefetch=1,
            grid=(4,),
            in_specs=[
                pl.BlockSpec(block, lambda i, y: (0, 4 * y[0] + i)),
                pl.BlockSpec(block, lambda i, y: (0, i)),
                pl.BlockSpec(block, lambda i, y: (0, i)),
                pl.BlockSpec(block, lambda i, y: (0, i)),
                whole(inner), whole(keep), whole(got1), whole(got2), whole(got3),
            ],
            out_specs=pl.BlockSpec((2, 288, 128), lambda i, y: (i, 0, 0)),
        ),
        out_shape=jax.ShapeDtypeStruct((NZ, 288, 128), BF16),
        name="down_product",
    )(my_y.reshape(1), saved, x1, x2, x3, inner, keep, got1, got2, got3)


def stages(
    section_inputs, adapter_down, adapter_up, representation, head_weights, head_targets, head_task
):
    my_x = lax.axis_index("x")
    my_c = lax.axis_index("c")
    my_y = lax.axis_index("y")
    my_dp = my_y * NZ + lax.axis_index("z")
    where = jnp.stack([my_x, my_c, my_y]).astype(jnp.int32)
    dim_model = section_inputs.shape[3]
    saved = section_inputs[0].reshape(-1, dim_model)
    down_map = adapter_down[0]
    up_map = adapter_up[0]
    heads = head_weights
    share, rank = heads.shape
    tok = representation.shape[1]
    column_task = jnp.repeat(head_task[:, 0], HEAD_OUT)
    mask = (column_task[None, :] == jnp.arange(rank, dtype=jnp.int32)[:, None]).astype(F32)

    piece = rows_at(heads, my_c * 128 + my_x * 32, 32)
    turn = [(a * NY + b, b * NY + a) for a in range(NX) for b in range(NY)]
    piece = lax.ppermute(piece, ("x", "y"), turn)

    blocks = representation[0].reshape(tok, NX, NZ, NC, 128).transpose(3, 1, 2, 0, 4)
    blocks = blocks.reshape(NC, NX, NZ * tok, 128)
    down_rows = rows_at(down_map, my_dp * share, share)
    swapped = swap_c(at(blocks, 1 - my_c))
    partner = swap_c(down_rows)
    pair = jnp.concatenate([at(blocks, my_c), swapped], axis=1)
    gots = []
    for k in range(1, NX):
        sent = jnp.concatenate([at(pair, (my_x - k) % NX), down_rows, partner], axis=0)
        gots.append(shift(sent, "x", -k))

    wide = dim_model // NY

    def cut(index, k, lo, size):
        return lax.dynamic_slice_in_dim(saved, ((index - k) % NY) * wide + lo, size, 1)

    x1 = cut(my_y, 1, 0, wide)
    x3 = cut(my_y, 3, 0, wide)
    x1, x3, tied_dp = lax.optimization_barrier((x1, x3, my_dp))
    x1 = shift(x1, "y", -1)
    x3 = shift(x3, "y", -3)

    up_rows = rows_at(up_map, tied_dp * share, share)
    sent, factors, rep = local_call(
        pack_kernel,
        [((DP, 64, rank), BF16), ((SECTIONS, share, rank), BF16), ((SECTIONS, NZ * tok, rank), BF16)],
        where, piece, heads, up_rows, at(pair, my_x), down_rows, partner, *gots,
    )

    late_y, down_late, sent = lax.optimization_barrier((my_y, down_map, sent))
    x2 = cut(late_y, 2, 0, wide)
    preact = jnp.dot(saved, down_late, preferred_element_type=F32)
    logistic = jax.nn.sigmoid(preact)
    active = (preact * logistic).astype(BF16)
    slope = (logistic * (1.0 + preact * (1.0 - logistic))).astype(BF16)
    slopes = [slope] + [from_later(slope, k) for k in range(1, NX)]
    slope_own = jnp.stack(slopes)
    slope_other = swap_c(slope_own)

    got = exchange_dp(sent)
    part, cross_rows, _ = local_call(
        heads_kernel,
        [((384, rank), F32), ((32, rank), BF16), ((1024, rank), BF16)],
        where, got, rep, head_targets[0],
    )
    got = exchange_dp(jnp.broadcast_to(cross_rows[None], (DP, 32, rank)))
    cross = got.reshape(-1, rank)
    kept = [cross]
    for k in range(1, NX):
        kept.append(from_later(cross[: LATER_ROWS[k]], k))
    part = part + swap_c(part)
    top = part.astype(BF16)
    low = (part[256:] - top[256:].astype(F32)).astype(BF16)
    halves = jnp.concatenate([top, low], axis=0)
    others = [shift(halves, "x", -k) for k in range(1, NX)]
    x2 = shift(x2, "y", -2)
    sent, residual = local_call(
        gram_kernel,
        [((DP, 16, rank), BF16), ((256, rank), BF16)],
        where, halves, *others, mask,
    )
    got = exchange_dp(sent)
    cross_own = jnp.concatenate(kept, axis=0)
    cross_other = swap_c(cross_own)
    keep, send1, send2, send3, inner, mix, _ = local_call(
        chain_kernel,
        [((256, rank), BF16)] + [((512, rank), BF16)] * 3
        + [((256, rank), BF16), ((8, rank), F32), ((1024, rank), BF16)],
        where, got, mask, residual, active, cross_own, cross_other, slope_own, slope_other,
    )
    got1 = shift(send1, "y", -1)
    got2 = shift(send2, "y", -2)
    got3 = shift(send3, "y", -3)
    part_down = run_down(my_y, saved, x1, x2, x3, inner, keep, got1, got2, got3)
    got = lax.all_to_all(part_down, "z", 0, 0, tiled=True)
    total = jnp.sum(got.astype(F32), axis=0)
    rows = total[256:].astype(BF16)
    middle = exchange_dp(jnp.broadcast_to(rows[None], (DP, 32, rank)))
    middle = middle.reshape(SECTIONS, rank, rank)
    grad_up = lax.dot_general(
        factors, middle, (((0, 2), (0, 2)), ((), ())), preferred_element_type=F32
    )
    grad_down = jnp.concatenate([total[:128].T, total[128:256].T], axis=0)
    return (grad_down[None], grad_up[None], mix[0, :TASKS])


def solution(mesh):
    fine = Mesh(mesh.devices.reshape(NX, NC, NY, NZ), ("x", "c", "y", "z"))
    section = ("x", "c")
    dp = ("y", "z")
    in_specs = (
        P(section, None, dp, None),
        P(section, None, None),
        P(section, None, None),
        P(section, dp, None),
        P(dp, None),
        P(section, dp, None),
        P(),
    )
    out_specs = (P(section, dp, None), P(section, dp, None), P())
    return jax.shard_map(stages, mesh=fine, in_specs=in_specs, out_specs=out_specs, check_vma=False)
```

```python
import jax
import jax.numpy as jnp
from jax import lax
from jax.experimental import pallas as pl
from jax.experimental.pallas import tpu as pltpu
from jax.sharding import Mesh
from jax.sharding import PartitionSpec as P


HEAD_OUT = 16
TASKS = 6
STEPS = 20
STEP_RATE = 3.0
NX = 4
NC = 2
NY = 4
NZ = 8
SECTIONS = NX * NC
DP = NY * NZ
BF16 = jnp.bfloat16
F32 = jnp.float32


def shift(value, axis, steps):
    count = lax.axis_size(axis)
    return lax.ppermute(value, axis, [(src, (src + steps) % count) for src in range(count)])


def from_later(value, steps):
    return lax.ppermute(value, "x", [(src, src - steps) for src in range(steps, NX)])


def swap_c(value):
    return lax.ppermute(value, "c", [(0, 1), (1, 0)])


def exchange_dp(blocks):
    return lax.all_to_all(blocks, ("y", "z"), 0, 0, tiled=True)


def at(value, index):
    return lax.dynamic_index_in_dim(value, index, 0, keepdims=False)


def rows_at(value, start, size):
    return lax.dynamic_slice_in_dim(value, start, size, 0)


def across(left, right):
    return lax.dot_general(left, right, (((0,), (0,)), ((), ())), preferred_element_type=F32)


VMEM = pl.BlockSpec(memory_space=pltpu.VMEM)
SMEM = pl.BlockSpec(memory_space=pltpu.SMEM)


def local_call(kernel, outs, where, *operands):
    return pl.pallas_call(
        kernel,
        out_shape=tuple(jax.ShapeDtypeStruct(shape, dtype) for shape, dtype in outs),
        in_specs=[SMEM] + [VMEM] * len(operands),
        out_specs=(VMEM,) * len(outs),
    )(where, *operands)


def pack_kernel(
    where_ref, piece_ref, heads_ref, up_ref, own_rep_ref, own_ref, partner_ref,
    got1_ref, got2_ref, got3_ref, sent_ref, factor_ref, rep_ref,
):
    my_x = where_ref[0]
    my_c = where_ref[1]
    my_stage = my_x * NC + my_c
    up_rows = up_ref[...]
    piece = piece_ref[...]
    for d in range(DP):
        sent_ref[d, 0:32, :] = piece
    gots = (None, got1_ref, got2_ref, got3_ref)
    for k in range(NX):
        for r in range(NC):
            stage = ((my_x + k) % NX) * NC + (my_c if r == 0 else 1 - my_c)
            slot = SECTIONS - 1 - stage
            if k == 0:
                rep_rows = own_rep_ref[256 * r : 256 * r + 256, :]
                factor = heads_ref[...] if r == 0 else partner_ref[...]
            else:
                rep_rows = gots[k][256 * r : 256 * r + 256, :]
                factor = gots[k][512 + 256 * r : 768 + 256 * r, :]
            if k or r:
                factor = jnp.where(stage > my_stage, factor, jnp.zeros_like(factor))
            rep_ref[stage] = rep_rows
            factor_ref[slot] = factor
            product = across(factor, up_rows).astype(BF16)
            for i in range(4):
                sent_ref[4 * slot + i, 32:64, :] = product[32 * i : 32 * i + 32]


def heads_kernel(where_ref, got_ref, rep_ref, target_ref, part_ref, cross_ref, head_ref):
    my_stage = where_ref[0] * NC + where_ref[1]
    for z in range(NZ):
        for y in range(NY):
            head_ref[128 * z + 32 * y : 128 * z + 32 * y + 32, :] = got_ref[NZ * y + z, 0:32, :]
    total = None
    square = None
    for z in range(NZ):
        head = head_ref[128 * z : 128 * z + 128, :]
        rep = jnp.concatenate([rep_ref[m, 32 * z : 32 * z + 32, :] for m in range(SECTIONS)], axis=0)
        term = jnp.dot(rep, head, preferred_element_type=F32)
        other = across(head, head)
        total = term if total is None else total + term
        square = other if square is None else square + other
    target = target_ref[...].astype(F32)
    for m in range(SECTIONS):
        rows = total[32 * m : 32 * m + 32]
        part_ref[32 * m : 32 * m + 32, :] = rows - jnp.where(m == my_stage, target, 0.0)
    part_ref[256:384, :] = square
    cross = jnp.sum(got_ref[:, 32:64, :].astype(F32), axis=0).astype(BF16)
    for d in range(DP):
        cross_ref[d] = cross


def gram_kernel(where_ref, a_ref, b_ref, c_ref, d_ref, mask_ref, sent_ref, residual_ref):
    def value(ref, lo, size):
        return ref[lo : lo + size, :].astype(F32)

    def summed(lo, size):
        pair = value(a_ref, lo, size) + value(c_ref, lo, size)
        return pair + (value(b_ref, lo, size) + value(d_ref, lo, size))

    def squares(ref):
        return value(ref, 256, 128) + value(ref, 384, 128)

    residual = summed(0, 256).astype(BF16)
    residual_ref[...] = residual
    square = (squares(a_ref) + squares(c_ref)) + (squares(b_ref) + squares(d_ref))
    product = square * across(residual, residual)
    mask = mask_ref[...]
    high = lax.Precision.HIGHEST
    half = jnp.dot(mask[0:8], product, precision=high, preferred_element_type=F32)
    part = lax.dot_general(
        half, mask, (((1,), (1,)), ((), ())), precision=high, preferred_element_type=F32
    )
    top = part.astype(BF16)
    tile = jnp.concatenate([part, part - top.astype(F32)], axis=0).astype(BF16)
    for d in range(DP):
        sent_ref[d] = tile


LATER_ROWS = (1024, 768, 512, 256)
LATER_FROM = (0, 1024, 1792, 2304)
ALL_ROWS = 2560


def chain_kernel(
    where_ref, got_ref, mask_ref, residual_ref, active_ref, own_ref, other_ref,
    slope_own_ref, slope_other_ref,
    keep_ref, send1_ref, send2_ref, send3_ref, inner_ref, mix_ref, middle_ref,
):
    my_x = where_ref[0]
    my_c = where_ref[1]
    my_y = where_ref[2]
    my_stage = my_x * NC + my_c
    tiles = jnp.sum(got_ref[...].astype(F32), axis=0)
    gram = tiles[0:8] + tiles[8:16]
    rows = lax.broadcasted_iota(jnp.int32, gram.shape, 0)
    lanes = lax.broadcasted_iota(jnp.int32, gram.shape, 1)
    diagonal = jnp.where(rows == lanes, gram, 0.0)
    trace_sum = jnp.sum(jnp.sum(diagonal, axis=1, keepdims=True), axis=0, keepdims=True) + 1e-06
    scaled = gram * (-STEP_RATE / trace_sum)
    tasks = range(TASKS)
    entry = [[jnp.broadcast_to(scaled[t : t + 1, u : u + 1], (8, 128)) for u in tasks] for t in tasks]

    def advance(counter, weights):
        total = ((weights[0] + weights[1]) + (weights[2] + weights[3])) + (weights[4] + weights[5])
        inverse = 1.0 / total
        moved = []
        for t in tasks:
            terms = [entry[t][u] * weights[u] for u in tasks]
            step = ((terms[0] + terms[1]) + (terms[2] + terms[3])) + (terms[4] + terms[5])
            moved.append(weights[t] * jnp.exp(step * inverse))
        return tuple(moved)

    even = jnp.full((8, 128), 1.0 / TASKS, F32)
    weights = lax.fori_loop(0, STEPS, advance, (even,) * TASKS)
    total = ((weights[0] + weights[1]) + (weights[2] + weights[3])) + (weights[4] + weights[5])
    weights = [weight / total for weight in weights]
    mix = jnp.zeros((8, 128), F32)
    column_weight = jnp.zeros((1, 128), F32)
    for t in tasks:
        mix = jnp.where(lanes == t, weights[t], mix)
        column_weight = column_weight + weights[t][0:1] * mask_ref[t : t + 1]
    mix_ref[...] = mix

    def cross(stage, source):
        away = (stage // NC - my_x) % NX
        start = jnp.where(away == 0, LATER_FROM[0], LATER_FROM[1])
        start = jnp.where(away == 2, LATER_FROM[2], start)
        start = jnp.where(away == 3, LATER_FROM[3], start)
        start = jnp.minimum(start + 128 * (SECTIONS - 1 - source), ALL_ROWS - 128)
        start = pl.multiple_of(start, 128)
        own = own_ref[pl.ds(start, 128), :]
        return jnp.where(my_c == stage % NC, own, other_ref[pl.ds(start, 128), :])

    def slope_of(stage):
        away = (stage // NC - my_x) % NX
        return jnp.where(my_c == stage % NC, slope_own_ref[away], slope_other_ref[away])

    active = active_ref[...].T
    weighted = (residual_ref[...].astype(F32) * column_weight).astype(BF16)
    first = jnp.dot(active, weighted, preferred_element_type=F32)
    inners = {}
    for stage in range(SECTIONS - 1, -1, -1):
        left = [weighted] + [inners[s] for s in range(SECTIONS - 1, stage, -1)]
        right = [cross(stage, s) for s in [stage] + list(range(SECTIONS - 1, stage, -1))]
        branch = None
        for n in range(0, len(left), 2):
            term = jnp.dot(
                jnp.concatenate(left[n : n + 2], axis=1),
                jnp.concatenate(right[n : n + 2], axis=0),
                preferred_element_type=F32,
            )
            branch = term if branch is None else branch + term
        inner = (branch * slope_of(stage).astype(F32)).astype(BF16)
        inners[stage] = inner

        @pl.when(stage == my_stage)
        def _():
            inner_ref[...] = inner
            send1_ref[256:512, :] = inner
            send2_ref[256:512, :] = inner
            send3_ref[256:512, :] = inner

        product = jnp.dot(active, inner, preferred_element_type=F32)
        product = jnp.where(stage > my_stage, product, 0.0)
        product = jnp.where(stage == my_stage, first, product)
        lo = 128 * (SECTIONS - 1 - stage)
        middle_ref[lo : lo + 128, :] = product.astype(BF16)

    for k, ref in enumerate((keep_ref, send1_ref, send2_ref, send3_ref)):
        start = pl.multiple_of(((my_y - k) % NY) * 256, 256)
        ref[0:256, :] = middle_ref[pl.ds(start, 256), :]


def down_kernel(
    y_ref, x0_ref, x1_ref, x2_ref, x3_ref, inner_ref, keep_ref, got1_ref, got2_ref, got3_ref,
    out_ref,
):
    step = pl.program_id(0)
    total = across(inner_ref[...], x0_ref[...])
    total = total + across(got1_ref[256:512, :], x1_ref[...])
    total = total + across(got2_ref[256:512, :], x2_ref[...])
    total = total + across(got3_ref[256:512, :], x3_ref[...])
    total = total.astype(BF16)
    for j in range(2):
        for h in range(2):
            lo = 256 * j + 128 * h
            out_ref[j, 128 * h : 128 * h + 128, :] = total[:, lo : lo + 128]
        start = pl.multiple_of((2 * step + j) * 32, 32)
        rows = [ref[pl.ds(start, 32), :].astype(F32) for ref in (keep_ref, got1_ref, got2_ref, got3_ref)]
        out_ref[j, 256:288, :] = ((rows[0] + rows[1]) + (rows[2] + rows[3])).astype(BF16)


def run_down(my_y, saved, x1, x2, x3, inner, keep, got1, got2, got3):
    cols = 512
    whole = lambda value: pl.BlockSpec(value.shape, lambda i, y: (0, 0))
    block = (256, cols)
    return pl.pallas_call(
        down_kernel,
        grid_spec=pltpu.PrefetchScalarGridSpec(
            num_scalar_prefetch=1,
            grid=(4,),
            in_specs=[
                pl.BlockSpec(block, lambda i, y: (0, 4 * y[0] + i)),
                pl.BlockSpec(block, lambda i, y: (0, i)),
                pl.BlockSpec(block, lambda i, y: (0, i)),
                pl.BlockSpec(block, lambda i, y: (0, i)),
                whole(inner), whole(keep), whole(got1), whole(got2), whole(got3),
            ],
            out_specs=pl.BlockSpec((2, 288, 128), lambda i, y: (i, 0, 0)),
        ),
        out_shape=jax.ShapeDtypeStruct((NZ, 288, 128), BF16),
        name="down_product",
    )(my_y.reshape(1), saved, x1, x2, x3, inner, keep, got1, got2, got3)


def stages(
    section_inputs, adapter_down, adapter_up, representation, head_weights, head_targets, head_task
):
    my_x = lax.axis_index("x")
    my_c = lax.axis_index("c")
    my_y = lax.axis_index("y")
    my_dp = my_y * NZ + lax.axis_index("z")
    where = jnp.stack([my_x, my_c, my_y]).astype(jnp.int32)
    dim_model = section_inputs.shape[3]
    saved = section_inputs[0].reshape(-1, dim_model)
    down_map = adapter_down[0]
    up_map = adapter_up[0]
    heads = head_weights
    share, rank = heads.shape
    tok = representation.shape[1]
    column_task = jnp.repeat(head_task[:, 0], HEAD_OUT)
    mask = (column_task[None, :] == jnp.arange(rank, dtype=jnp.int32)[:, None]).astype(F32)

    piece = rows_at(heads, my_c * 128 + my_x * 32, 32)
    turn = [(a * NY + b, b * NY + a) for a in range(NX) for b in range(NY)]
    piece = lax.ppermute(piece, ("x", "y"), turn)

    blocks = representation[0].reshape(tok, NX, NZ, NC, 128).transpose(3, 1, 2, 0, 4)
    blocks = blocks.reshape(NC, NX, NZ * tok, 128)
    down_rows = rows_at(down_map, my_dp * share, share)
    swapped = swap_c(at(blocks, 1 - my_c))
    partner = swap_c(down_rows)
    pair = jnp.concatenate([at(blocks, my_c), swapped], axis=1)
    gots = []
    for k in range(1, NX):
        sent = jnp.concatenate([at(pair, (my_x - k) % NX), down_rows, partner], axis=0)
        gots.append(shift(sent, "x", -k))

    wide = dim_model // NY

    def cut(index, k, lo, size):
        return lax.dynamic_slice_in_dim(saved, ((index - k) % NY) * wide + lo, size, 1)

    x1 = cut(my_y, 1, 0, wide)
    x3 = cut(my_y, 3, 0, wide)
    x1, x3, tied_dp = lax.optimization_barrier((x1, x3, my_dp))
    x1 = shift(x1, "y", -1)
    x3 = shift(x3, "y", -3)

    up_rows = rows_at(up_map, tied_dp * share, share)
    sent, factors, rep = local_call(
        pack_kernel,
        [((DP, 64, rank), BF16), ((SECTIONS, share, rank), BF16), ((SECTIONS, NZ * tok, rank), BF16)],
        where, piece, heads, up_rows, at(pair, my_x), down_rows, partner, *gots,
    )

    late_y, down_late, sent = lax.optimization_barrier((my_y, down_map, sent))
    x2 = cut(late_y, 2, 0, wide)
    preact = jnp.dot(saved, down_late, preferred_element_type=F32)
    logistic = jax.nn.sigmoid(preact)
    active = (preact * logistic).astype(BF16)
    slope = (logistic * (1.0 + preact * (1.0 - logistic))).astype(BF16)
    slopes = [slope] + [from_later(slope, k) for k in range(1, NX)]
    slope_own = jnp.stack(slopes)
    slope_other = swap_c(slope_own)

    got = exchange_dp(sent)
    part, cross_rows, _ = local_call(
        heads_kernel,
        [((384, rank), F32), ((DP, 32, rank), BF16), ((1024, rank), BF16)],
        where, got, rep, head_targets[0],
    )
    got = exchange_dp(cross_rows)
    cross = got.reshape(-1, rank)
    kept = [cross]
    for k in range(1, NX):
        kept.append(from_later(cross[: LATER_ROWS[k]], k))
    part = part + swap_c(part)
    top = part.astype(BF16)
    low = (part[256:] - top[256:].astype(F32)).astype(BF16)
    halves = jnp.concatenate([top, low], axis=0)
    others = [shift(halves, "x", -k) for k in range(1, NX)]
    x2 = shift(x2, "y", -2)
    sent, residual = local_call(
        gram_kernel,
        [((DP, 16, rank), BF16), ((256, rank), BF16)],
        where, halves, *others, mask,
    )
    got = exchange_dp(sent)
    cross_own = jnp.concatenate(kept, axis=0)
    cross_other = swap_c(cross_own)
    keep, send1, send2, send3, inner, mix, _ = local_call(
        chain_kernel,
        [((256, rank), BF16)] + [((512, rank), BF16)] * 3
        + [((256, rank), BF16), ((8, rank), F32), ((1024, rank), BF16)],
        where, got, mask, residual, active, cross_own, cross_other, slope_own, slope_other,
    )
    got1 = shift(send1, "y", -1)
    got2 = shift(send2, "y", -2)
    got3 = shift(send3, "y", -3)
    part_down = run_down(my_y, saved, x1, x2, x3, inner, keep, got1, got2, got3)
    got = lax.all_to_all(part_down, "z", 0, 0, tiled=True)
    total = jnp.sum(got.astype(F32), axis=0)
    rows = total[256:].astype(BF16)
    middle = exchange_dp(jnp.broadcast_to(rows[None], (DP, 32, rank)))
    middle = middle.reshape(SECTIONS, rank, rank)
    grad_up = lax.dot_general(
        factors, middle, (((0, 2), (0, 2)), ((), ())), preferred_element_type=F32
    )
    grad_down = jnp.concatenate([total[:128].T, total[128:256].T], axis=0)
    return (grad_down[None], grad_up[None], mix[0, :TASKS])


def solution(mesh):
    fine = Mesh(mesh.devices.reshape(NX, NC, NY, NZ), ("x", "c", "y", "z"))
    section = ("x", "c")
    dp = ("y", "z")
    in_specs = (
        P(section, None, dp, None),
        P(section, None, None),
        P(section, None, None),
        P(section, dp, None),
        P(dp, None),
        P(section, dp, None),
        P(),
    )
    out_specs = (P(section, dp, None), P(section, dp, None), P())
    return jax.shard_map(stages, mesh=fine, in_specs=in_specs, out_specs=out_specs, check_vma=False)
```
